128 devices in a mesh: dom: 128 (over z, y, x, core).
Axes of the slice: x: 4, y: 4, z: 4, core: 2. Of those that a mesh axis runs over, the one named last changes fastest.
Arguments:
- right_side: float32 [64, 16384], P(None, 'dom'), may hold values from -8 to 8
- sigma: float32 [64, 16384], P(None, 'dom'), may hold values from 0.5 to 2
- reluctivity: float32 [64, 16384], P(None, 'dom'), may hold values from 0.2 to 5
- curl_blocks: float32 [6, 64, 64, 16384], P(None, None, None, 'dom'), may hold values from -0.3125 to 0.3125
- pattern: int32 [6, 16384], P(None, 'dom'), may hold values from 0 to 191
- cond_weight: float32 [64, 65536], P(None, 'dom'), may hold values from -0.125 to 0.125
- cond_block: int32 [65536], P('dom'), may hold values from 0 to 127
- cond_coil: int32 [65536, 1], P('dom'), may hold values from 0 to 83; in each aligned block of 512 rows (0 to 511, 512 to 1023, ...) at most 16 rows name the same one
- coil_phase: int32 [84], replicated, may hold values from 0 to 3
- coil_resistance: float32 [84], replicated, may hold values from 0.5 to 2
- switch_state: int32 [3], replicated, may hold values from 0 to 1
Outputs:
- solution_field: float32 [64, 16384], P(None, 'dom')
- residual: float32 [64, 16384], P(None, 'dom')
The draws below stay inside these ranges and needn't reach their ends.
Inputs may be any that keep to these rules, and one draw needn't show every extreme that they name: `cond_coil`: no coil is named by more than 16 of one partition's 512 conductor rows, a bound that some block reaches.
All inputs are finite; a program needn't handle non-finite values.
Results may differ from the reference program's by a relative error of at most 0.00055.
Values sent between devices are 32-bit elements; how exact they have to be, the bound alone decides.
No kernel may reach another device: no remote copies, remote signals or barrier semaphores. Data moves between devices by JAX's collectives and lax.ppermute only.
A program may use at most 64 MiB of HBM per device.

```python
import math
import jax
import jax.numpy as jnp
import numpy as np
from jax import lax

BS = 64
KB = 6
NB = 128
HALO = 32
BLOCKS = 16384
NC = 512
CAP = 16
COND = 65536
NCOIL = 84
NPH = 3
ITERS = 3
N_DOM = 128


def with_ends(array, rng, least, largest):
    shape = array.shape
    index_at = [jax.random.randint(jax.random.fold_in(rng, axis), (), 0, shape[axis]) for axis in range(len(shape))]
    array = array.at[tuple(index_at)].set(least)
    longest = shape.index(max(shape))
    index_at[longest] = (index_at[longest] + 1) % shape[longest]
    return array.at[tuple(index_at)].set(largest)


def levels(key, extent, cuts, least, largest):
    gain = 1.0
    for dim, shards_of in cuts:
        heights = jax.random.uniform(jax.random.fold_in(jax.random.fold_in(key, 6), dim), (shards_of,), jnp.float32, least / len(cuts), largest / len(cuts))
        gain = gain * jnp.repeat(jnp.exp(heights), extent[dim] // shards_of).reshape((-1,) + (1,) * (len(extent) - 1 - dim))
    return gain


def assign_block(rng, own, number, rows, count, top, bound, skew):
    sequence = jax.random.permutation(rng, count)
    packed, usual = load_shares(count, rows * top, bound, skew, True), load_shares(count, rows * top, bound, skew, False)
    places = jnp.arange(count)

    def named(tallies, rotation):
        used = int((tallies > 0).sum())
        fixed = max(1, used // 4)
        shifted = fixed + (places - fixed + rotation * (used - fixed)) % max(1, count - fixed)
        return jnp.zeros((count,), jnp.int32).at[sequence[jnp.where(places < fixed, places, shifted)]].set(jnp.asarray(tallies, jnp.int32))

    tallies = jnp.where(number % 4 == 0, named(packed, number // 4), named(usual, number - number // 4 - 1))
    mixed = jax.random.permutation(jax.random.fold_in(own, 3), count)
    donor, sink = mixed[0:count // 2 * 2:2], mixed[1:count // 2 * 2:2]
    slack = jnp.minimum(tallies[donor] - 1, bound - tallies[sink]) // 2
    slack = jnp.where((donor == sequence[0]) | (sink == sequence[0]) | (tallies[sink] == 0), 0, jnp.maximum(slack, 0))
    shifted = jax.random.randint(jax.random.fold_in(own, 4), (count // 2,), 0, 1 << 20) % (slack + 1)
    tallies = tallies.at[donor].add(-shifted).at[sink].add(shifted)
    labels = jnp.searchsorted(jnp.cumsum(tallies), jnp.arange(rows * top), side="right").astype(jnp.int32)
    grid = labels.reshape(top, rows).T
    grid = grid[jax.random.permutation(jax.random.fold_in(own, 1), rows)]
    rotation = jax.random.randint(jax.random.fold_in(own, 2), (rows, 1), 0, top)
    return jnp.take_along_axis(grid, (jnp.arange(top)[None, :] + rotation) % top, axis=1)


def load_shares(amount, total, most, lean, full):
    portions = [(1 << 20) // math.isqrt(rank ** lean) + 1 for rank in range(1, amount + 1)]
    largest = most if full else min(most, max(-(-total // amount), total * portions[0] // sum(portions)))
    least = 1 if total - largest >= amount - 1 else 0
    counts, spare = [largest] + [least] * (amount - 1), total - largest - least * (amount - 1)
    while spare > 0:
        free = [i for i in range(1, amount) if counts[i] < largest] or [i for i in range(1, amount) if counts[i] < most]
        whole, budget = sum([portions[i] for i in free]), spare
        for i in free:
            more = min(most - counts[i], max(1, budget * portions[i] // whole), spare)
            counts[i] = counts[i] + more
            spare = spare - more
    return np.array(counts)


def noise(own_key, shape, scale, limit, split=(), kind=jnp.bfloat16):
    values = scale * jax.random.normal(own_key, shape, jnp.float32)
    if split:
        values = values * levels(own_key, shape, split, -0.22, 0.18)
    return jnp.clip(values, -limit, limit).astype(kind)


def setup_inputs(seed: int = 0) -> dict:
    seeds = jax.random.split(jax.random.key(seed), 12)
    right_side = noise(seeds[0], (BS, BLOCKS), 1.0, 8.0, ((1, 128),), jnp.float32)
    sigma = jnp.clip(jnp.exp(math.log(2.0) - 1.3862944 * jax.random.uniform(seeds[1], (BS, BLOCKS), jnp.float32) ** levels(seeds[1], (BS, BLOCKS), ((1, 128),), -0.2, 0.2)), 0.5, 2.0)
    reluctivity = jnp.clip(jnp.exp(math.log(5.0) - 3.218876 * jax.random.uniform(seeds[2], (BS, BLOCKS), jnp.float32) ** levels(seeds[2], (BS, BLOCKS), ((1, 128),), -0.2, 0.2)), 0.2, 5.0)
    curl_blocks = noise(seeds[3], (KB, BS, BS, BLOCKS), (BS * KB) ** -0.5, 0.3125, ((3, 128),), jnp.float32)
    pattern = with_ends(jax.random.randint(seeds[4], (KB, BLOCKS), 0, NB + 2 * HALO), jax.random.fold_in(seeds[4], 1), 0, (NB + 2 * HALO) - 1).astype(jnp.int32)
    cond_weight = noise(seeds[5], (BS, COND), (COND * 16 // (5 * NCOIL)) ** -0.5, 0.125, ((1, 128),), jnp.float32)
    cond_block = with_ends(jax.random.randint(seeds[6], (COND,), 0, NB), jax.random.fold_in(seeds[6], 1), 0, NB - 1).astype(jnp.int32)
    cond_coil_keys = jax.random.split(jax.random.fold_in(seeds[7], 1), COND // NC)
    cond_coil_turns = jax.random.permutation(jax.random.fold_in(seeds[7], 3), COND // NC)
    cond_coil = jax.vmap(lambda own, number: assign_block(jax.random.fold_in(seeds[7], 2), own, number, NC, NCOIL, 1, CAP, 2))(cond_coil_keys, cond_coil_turns).reshape((COND, 1))
    coil_phase = with_ends(jax.random.randint(seeds[8], (NCOIL,), 0, NPH + 1), jax.random.fold_in(seeds[8], 1), 0, NPH).astype(jnp.int32)
    coil_resistance = jnp.clip(jnp.exp(jax.random.uniform(seeds[9], (NCOIL,), jnp.float32, math.log(0.5), math.log(2.0))), 0.5, 2.0)
    switch_state = jax.random.randint(seeds[10], (NPH,), 0, 2).astype(jnp.int32)
    return {"right_side": right_side, "sigma": sigma, "reluctivity": reluctivity, "curl_blocks": curl_blocks, "pattern": pattern, "cond_weight": cond_weight, "cond_block": cond_block, "cond_coil": cond_coil, "coil_phase": coil_phase, "coil_resistance": coil_resistance, "switch_state": switch_state}


link_scale = 16.0


def reference(right_side, sigma, reluctivity, curl_blocks, pattern, cond_weight, cond_block, cond_coil, coil_phase, coil_resistance, switch_state):
    width = right_side.shape[0]
    total_blocks = right_side.shape[1]
    block_count = total_blocks // N_DOM
    halo_width = block_count // 4
    row_total = cond_block.shape[0]
    row_count = row_total // N_DOM
    coil_rows = cond_coil[:, 0]
    gblock = (cond_block + (jnp.arange(row_total, dtype=jnp.int32) // row_count) * block_count).astype(jnp.int32)
    switch_float = switch_state.astype(jnp.float32)
    table = jnp.concatenate([switch_float - jnp.mean(switch_float), jnp.zeros((1,), jnp.float32)])
    coil_volts = link_scale * table[coil_phase]
    row_source = (coil_volts / coil_resistance)[coil_rows]
    rhs = right_side + jnp.zeros_like(right_side).at[:, gblock].add(cond_weight * row_source[None, :])

    def operate(field):
        padded = jnp.pad(field, ((0, 0), (halo_width, halo_width)))

        def one_part(domain):
            start = (domain * block_count).astype(jnp.int32)
            window = lax.dynamic_slice_in_dim(padded, start, block_count + 2 * halo_width, 1)
            blocks = lax.dynamic_slice_in_dim(curl_blocks, start, block_count, 3)
            columns = lax.dynamic_slice_in_dim(pattern, start, block_count, 1)
            weights = lax.dynamic_slice_in_dim(reluctivity, start, block_count, 1)
            picked = window[:, columns]
            face_flux = jnp.einsum("kabn,bkn->an", blocks, picked, precision=lax.Precision.HIGHEST)
            back_terms = jnp.einsum("kabn,an->bkn", blocks, weights * face_flux, precision=lax.Precision.HIGHEST)
            return jnp.zeros_like(window).at[:, columns].add(back_terms)

        spreads = lax.map(one_part, jnp.arange(N_DOM, dtype=jnp.int32))
        centre = spreads[:, :, halo_width:halo_width + block_count]
        left_rims = spreads[:, :, :halo_width]
        right_rims = spreads[:, :, halo_width + block_count:]
        centre = centre.at[:-1, :, block_count - halo_width:].add(left_rims[1:])
        centre = centre.at[1:, :, :halo_width].add(right_rims[:-1])
        back_field = jnp.transpose(centre, (1, 0, 2)).reshape(width, total_blocks)
        partial_link = jnp.sum(cond_weight * field[:, gblock], axis=0)
        linkage = jnp.zeros((coil_resistance.shape[0],), jnp.float32).at[coil_rows].add(partial_link)
        currents = linkage / coil_resistance
        coupled = jnp.zeros_like(field).at[:, gblock].add(cond_weight * currents[coil_rows][None, :])
        return sigma * field + back_field + coupled

    solution_field = jnp.zeros_like(rhs)
    residual, direction = rhs, rhs
    norm_now = jnp.sum(residual * residual)
    for turn_index in range(ITERS):
        image = operate(direction)
        alpha = norm_now / jnp.sum(direction * image)
        solution_field = solution_field + alpha * direction
        residual = residual - alpha * image
        norm_next = jnp.sum(residual * residual)
        direction = residual + (norm_next / norm_now) * direction
        norm_now = norm_next
    return solution_field, residual
```

```python
import functools

import jax
import jax.numpy as jnp
from jax import lax
from jax.experimental import pallas as pl
from jax.experimental.pallas import tpu as pltpu
from jax.sharding import PartitionSpec as P

ITERS = 3
LINK_SCALE = 16.0
LANES = 128
F32 = jnp.float32
BF16 = jnp.bfloat16
VMEM = pltpu.VMEM


def gather_lanes(x, idx):
    dims = lax.GatherDimensionNumbers(
        offset_dims=(),
        collapsed_slice_dims=(1,),
        start_index_map=(1,),
        operand_batching_dims=(0,),
        start_indices_batching_dims=(0,),
    )
    return lax.gather(
        x,
        idx[..., None],
        dims,
        slice_sizes=(1, 1),
        mode=lax.GatherScatterMode.PROMISE_IN_BOUNDS,
    )


def lane_iota(rows=1, lanes=LANES):
    return lax.broadcasted_iota(jnp.int32, (rows, lanes), 1)


def nt_dot(a, b):
    return lax.dot_general(a, b, (((1,), (1,)), ((), ())), preferred_element_type=F32)


def split_rows(x):
    high = x.astype(BF16)
    low = (x - high.astype(F32)).astype(BF16)
    return jnp.concatenate([high, low], axis=0)


def add_halves(x):
    half = x.shape[0] // 2
    return x[:half] + x[half:]


def rows_of(ids):
    return jnp.concatenate([ids[i : i + 1] for i in range(ids.shape[0])], axis=1)


def onehot(ids, count):
    slots = lax.broadcasted_iota(jnp.int32, (count, ids.shape[1]), 0)
    return jnp.where(slots == ids, 1.0, 0.0).astype(BF16)


def weighted(weight, table, coils):
    parts = []
    wide = jnp.broadcast_to(table, (8, LANES))
    for i in range(coils.shape[1] // LANES):
        tile = coils[:, i * LANES : (i + 1) * LANES]
        got = gather_lanes(wide, jnp.broadcast_to(tile, (8, LANES)))
        cut = weight[:, i * LANES : (i + 1) * LANES]
        parts.append(cut * jnp.broadcast_to(got[0:1], cut.shape))
    return jnp.concatenate(parts, axis=1)


def pad_lanes(row, scratch):
    scratch[...] = jnp.zeros_like(scratch)
    scratch[0:1, 0 : row.shape[1]] = row
    return scratch[0:1, :]


def rhs_kernel(
    side_ref, weight_ref, block_ref, coil_ref, phase_ref, ohm_ref, state_ref, rhs_ref, pad_ref
):
    s0, s1, s2 = (state_ref[i].astype(F32) for i in range(3))
    mean = (s0 + s1 + s2) / 3.0
    phase = phase_ref[...]
    volts = jnp.where(
        phase == 0,
        s0 - mean,
        jnp.where(phase == 1, s1 - mean, jnp.where(phase == 2, s2 - mean, 0.0)),
    )
    source = pad_lanes(LINK_SCALE * volts / ohm_ref[...], pad_ref)
    coils, blocks = rows_of(coil_ref[...]), rows_of(block_ref[...])
    spread = split_rows(weighted(weight_ref[...], source, coils))
    rhs_ref[...] = side_ref[...] + add_halves(nt_dot(spread, onehot(blocks, LANES)))


def table_kernel(pattern_ref, block_ref, coil_ref, ohm_ref, pat_ref, blk_ref, coil_hot_ref, inv_ref):
    for k in range(pattern_ref.shape[0]):
        q = pattern_ref[k : k + 1, :]
        slot = jnp.where(q < 32, q + 128, jnp.where(q < 160, q - 32, q))
        pat_ref[:, k * LANES : (k + 1) * LANES] = onehot(slot, 2 * LANES)
    blk_ref[...] = onehot(rows_of(block_ref[...]), LANES)
    coil_hot_ref[...] = onehot(rows_of(coil_ref[...]), LANES)
    inv_ref[...] = jnp.zeros_like(inv_ref)
    inv_ref[0:1, 0 : ohm_ref.shape[1]] = 1.0 / ohm_ref[...]


def sides(a, b):
    even = lax.rem(lax.axis_index("dom"), 2) == 0
    return jnp.where(even, b, a), jnp.where(even, a, b)


def halo_mask(count):
    me = lax.axis_index("dom")
    lane = lane_iota()
    left = jnp.where(me > 0, 1.0, 0.0)
    right = jnp.where(me < count - 1, 1.0, 0.0)
    return jnp.where(lane < 32, left, jnp.where(lane < 64, right, 0.0))


def halo_of(left, right, count):
    lane = lane_iota(*left.shape)
    moved = jnp.where(lane < 32, pltpu.roll(left, 32, 1), pltpu.roll(right, 32, 1))
    return moved * halo_mask(count)


def apply_local(refs, own, halo, previous, row_out, msg_out, centre_out, rim_out, scratch):
    (sigma_ref, reluct_ref, curl_ref, pattern_ref, weight_ref, block_ref, coil_ref,
     pat_ref, coil_hot_ref) = refs
    picked_ref, face_ref, back_ref = scratch
    width = own.shape[0]
    rows = curl_ref.shape[1]
    kinds = pattern_ref.shape[0]

    for k in range(kinds):
        q = pattern_ref[k : k + 1, :]
        inside = jnp.logical_and(q >= 32, q < 160)
        idx = jnp.where(q < 32, q, jnp.where(inside, q - 32, q - 128))
        idx = jnp.broadcast_to(idx, (width, LANES))
        inside = jnp.broadcast_to(inside, (width, LANES))
        picked_ref[k] = jnp.where(inside, gather_lanes(own, idx), gather_lanes(halo, idx))

    @pl.loop(0, rows // 8)
    def _(step):
        first = pl.multiple_of(step * 8, 8)
        total = None
        for k in range(kinds):
            for t in range(0, width, 8):
                term = curl_ref[k, pl.ds(first, 8), t : t + 8, :] * picked_ref[k, t : t + 8, :][None]
                total = term if total is None else total + term
        face_ref[pl.ds(first, 8), :] = jnp.sum(total, axis=1)

    face = face_ref[...]
    bent = reluct_ref[...] * face
    energy = jnp.sum(bent * face + sigma_ref[...] * own * own, axis=0, keepdims=True)
    face_ref[...] = bent

    @pl.loop(0, kinds)
    def _(k):
        total = curl_ref[k, 0] * face_ref[0:1, :]
        for a in range(1, rows):
            total = total + curl_ref[k, a] * face_ref[a : a + 1, :]
        back_ref[:, pl.ds(pl.multiple_of(k * LANES, LANES), LANES)] = split_rows(total)

    spread = add_halves(nt_dot(back_ref[...], pat_ref[...]))
    rim = spread[:, LANES:]
    centre = sigma_ref[...] * own + spread[:, :LANES]
    centre_out[...] = centre
    rim_out[...] = rim
    lane = lane_iota(width)
    edges = jnp.logical_or(lane < 32, lane >= 96)
    msg_out[0:width, 0:LANES] = jnp.where(
        edges, centre, jnp.where(lane < 64, rim, pltpu.roll(rim, 64, 1))
    )

    links = []
    for i in range(block_ref.shape[0]):
        idx = jnp.broadcast_to(block_ref[i : i + 1, :], (width, LANES))
        got = gather_lanes(own, idx) * weight_ref[:, i * LANES : (i + 1) * LANES]
        links.append(jnp.sum(got, axis=0, keepdims=True))
    link = jnp.concatenate(links, axis=1)
    high = link.astype(BF16).astype(F32)
    mid = (link - high).astype(BF16).astype(F32)
    low = link - high - mid
    sub = lax.broadcasted_iota(jnp.int32, (8, link.shape[1]), 0)
    terms = jnp.where(sub == 0, high, jnp.where(sub == 1, mid, jnp.where(sub == 2, low, 0.0)))
    linkage = jnp.sum(nt_dot(terms.astype(BF16), coil_hot_ref[...]), axis=0, keepdims=True)

    coils = 84
    lane = lane_iota()
    norm = jnp.sum(jnp.sum(own * own, axis=0, keepdims=True), axis=1, keepdims=True)
    energy = jnp.sum(energy, axis=1, keepdims=True)
    line = linkage + jnp.where(lane == coils, norm, 0.0) + jnp.where(lane == coils + 1, energy, 0.0)
    if previous is not None:
        cross = jnp.sum(jnp.sum(own * previous, axis=0, keepdims=True), axis=1, keepdims=True)
        line = line + jnp.where(lane == coils + 2, cross, 0.0)
    row_out[...] = jnp.broadcast_to(line, row_out.shape)


def pick(line, at):
    return jnp.sum(jnp.where(lane_iota() == at, line, 0.0), axis=1, keepdims=True)


def first_kernel(count, rhs_ref, even_ref, odd_ref, sigma_ref, reluct_ref, curl_ref, pattern_ref,
                 weight_ref, block_ref, coil_ref, pat_ref, coil_hot_ref,
                 row_ref, msg_ref, centre_ref, rim_ref, halo_ref, *scratch):
    left, right = sides(even_ref[...], odd_ref[...])
    halo = halo_of(left, right, count)
    halo_ref[...] = halo
    width = rhs_ref.shape[0]
    msg_ref[0:width, LANES:] = weight_ref[...]
    msg_ref[width:, :] = jnp.zeros_like(msg_ref[width:, :])
    msg_ref[width : width + 1, LANES:] = rows_of(block_ref[...]).astype(F32)
    msg_ref[width + 1 : width + 2, LANES:] = rows_of(coil_ref[...]).astype(F32)
    refs = (sigma_ref, reluct_ref, curl_ref, pattern_ref, weight_ref, block_ref, coil_ref,
            pat_ref, coil_hot_ref)
    apply_local(refs, rhs_ref[...], halo, None, row_ref, msg_ref, centre_ref, rim_ref, scratch)


def scalars(rows_ref, inv_ref, scal_ref):
    coils = 84
    total = jnp.sum(rows_ref[...], axis=0, keepdims=True)
    current = total * inv_ref[0:1, :]
    norm, energy = pick(total, coils), pick(total, coils + 1)
    energy = energy + jnp.sum(current * total, axis=1, keepdims=True)
    if scal_ref is None:
        beta = None
        curve = energy
    else:
        beta = norm / pick(scal_ref[0:1, :], 0)
        cross = pick(total, coils + 2)
        curve = energy + 2.0 * beta * cross + beta * beta * pick(scal_ref[0:1, :], 1)
    lane = lane_iota()
    state = jnp.where(lane == 0, norm, jnp.where(lane == 1, curve, 0.0))
    return current, norm / curve, beta, state


def own_image(left, right, centre, weight, current, coils, blk):
    lane = lane_iota(*centre.shape)
    image = centre + jnp.where(lane < 32, pltpu.roll(left, 96, 1), 0.0)
    image = image + jnp.where(lane >= 96, pltpu.roll(right, 32, 1), 0.0)
    return image + add_halves(nt_dot(split_rows(weighted(weight, current, coils)), blk))


def step_kernel(count, first, *refs):
    names = ["rows", "even", "odd"] + ([] if first else ["evenc", "oddc"])
    names += ["centre", "rim", "res", "halo"] + ([] if first else ["dir", "img", "imgh", "sol", "scal"])
    names += ["inv", "blk", "sigma", "reluct", "curl", "pattern", "weight", "block", "coil", "pat",
              "coilhot"]
    names += ["row_o", "msg_o", "centre_o", "rim_o", "res_o", "halo_o", "dir_o", "img_o", "imgh_o",
              "sol_o", "scal_o"]
    r = dict(zip(names, refs))
    scratch = refs[len(names):]
    width = r["res"].shape[0]
    current, alpha, beta, state = scalars(r["rows"], r["inv"], r.get("scal"))
    r["scal_o"][...] = jnp.broadcast_to(state, r["scal_o"].shape)

    left, right = sides(r["even"][0:width, 0:LANES], r["odd"][0:width, 0:LANES])
    image = own_image(left, right, r["centre"][...], r["weight"][...], current,
                      rows_of(r["coil"][...]), r["blk"][...])

    ce, co = (r["even"], r["odd"]) if first else (r["evenc"], r["oddc"])
    cl, cr = sides(ce[:, LANES:], co[:, LANES:])
    spot = jnp.concatenate(
        [cl[width : width + 1].astype(jnp.int32) - 96, cr[width : width + 1].astype(jnp.int32) + 32],
        axis=1,
    )
    amount = jnp.concatenate(
        [
            weighted(c[0:width], current, c[width + 1 : width + 2].astype(jnp.int32))
            for c in (cl, cr)
        ],
        axis=1,
    )
    beyond = add_halves(nt_dot(split_rows(amount), onehot(spot, LANES)))
    lane = lane_iota(width)
    moved = jnp.where(lane < 32, pltpu.roll(left, 32, 1), pltpu.roll(right, 32, 1))
    image_halo = (moved + r["rim"][...] + beyond) * halo_mask(count)

    old = r["res"][...]
    if first:
        direction = old
        r["sol_o"][...] = alpha * direction
    else:
        direction = old + beta * r["dir"][...]
        image = image + beta * r["img"][...]
        image_halo = image_halo + beta * r["imgh"][...]
        r["sol_o"][...] = r["sol"][...] + alpha * direction
    r["dir_o"][...] = direction
    r["img_o"][...] = image
    r["imgh_o"][...] = image_halo
    own = old - alpha * image
    halo = r["halo"][...] - alpha * image_halo
    r["res_o"][...] = own
    r["halo_o"][...] = halo
    refs = tuple(r[k] for k in ("sigma", "reluct", "curl", "pattern", "weight", "block", "coil", "pat",
                                "coilhot"))
    apply_local(refs, own, halo, image, r["row_o"], r["msg_o"], r["centre_o"], r["rim_o"], scratch)


def last_kernel(rows_ref, even_ref, odd_ref, centre_ref, res_ref, dir_ref, img_ref, sol_ref, scal_ref,
                inv_ref, blk_ref, weight_ref, coil_ref, sol_out, res_out):
    current, alpha, beta, _ = scalars(rows_ref, inv_ref, scal_ref)
    left, right = sides(even_ref[...], odd_ref[...])
    image = own_image(left, right, centre_ref[...], weight_ref[...], current,
                      rows_of(coil_ref[...]), blk_ref[...])
    image = image + beta * img_ref[...]
    sol_out[...] = sol_ref[...] + alpha * (res_ref[...] + beta * dir_ref[...])
    res_out[...] = res_ref[...] - alpha * image


def call(kernel, args, outs, name, smem=(), scratch=()):
    return pl.pallas_call(
        kernel,
        name=name,
        in_specs=[
            pl.BlockSpec(memory_space=pltpu.SMEM if i in smem else VMEM) for i in range(len(args))
        ],
        out_specs=[pl.BlockSpec(memory_space=VMEM)] * len(outs),
        out_shape=[jax.ShapeDtypeStruct(s, d) for s, d in outs],
        scratch_shapes=list(scratch),
        compiler_params=pltpu.CompilerParams(vmem_limit_bytes=24 << 20),
    )(*args)


def body(count, right_side, sigma, reluctivity, curl_blocks, pattern, cond_weight, cond_block,
         cond_coil, coil_phase, coil_resistance, switch_state):
    width, blocks = right_side.shape
    kinds = pattern.shape[0]
    conductors = cond_weight.shape[1]
    block = cond_block.reshape(-1, LANES)
    coil = cond_coil.reshape(-1, LANES)
    phase = coil_phase.reshape(1, -1)
    ohm = coil_resistance.reshape(1, -1)
    tile = ((width, LANES), F32)

    inner = [(i, i ^ 1) for i in range(count)]
    outer = [(i, i + 1) for i in range(1, count - 1, 2)]
    outer = outer + [(b, a) for a, b in outer]

    def exchange(message):
        return lax.ppermute(message, "dom", outer), lax.ppermute(message, "dom", inner)

    def gather_rows(rows):
        return lax.all_to_all(rows, "dom", 0, 0, tiled=True)

    (rhs,) = call(
        rhs_kernel,
        (right_side, cond_weight, block, coil, phase, ohm, switch_state),
        [tile],
        "rhs",
        smem=(6,),
        scratch=[VMEM((8, LANES), F32)],
    )
    odd, even = exchange(rhs)
    pat, blk, coil_hot, inv = call(
        table_kernel,
        (pattern, block, coil, ohm),
        [((2 * LANES, kinds * LANES), BF16), ((LANES, conductors), BF16),
         ((LANES, conductors), BF16), ((8, LANES), F32)],
        "tables",
    )
    scratch = [VMEM((kinds, width, LANES), F32), VMEM((width, LANES), F32),
               VMEM((2 * width, kinds * LANES), BF16)]
    shared = (sigma, reluctivity, curl_blocks, pattern, cond_weight, block, coil, pat, coil_hot)
    line = ((count, LANES), F32)
    wide = ((width + 8, LANES + conductors), F32)
    row, message, centre, rim, halo = call(
        functools.partial(first_kernel, count),
        (rhs, even, odd) + shared,
        [line, wide, tile, tile, tile],
        "apply0",
        scratch=scratch,
    )
    odd_c, even_c = odd, even = exchange(message)
    rows = gather_rows(row)
    state = [line, tile, tile, tile, tile, tile, tile, tile, tile, tile, ((8, LANES), F32)]
    row, message, centre, rim, res, halo, direction, image, image_halo, sol, scal = call(
        functools.partial(step_kernel, count, True),
        (rows, even, odd, centre, rim, rhs, halo, inv, blk) + shared,
        state,
        "apply1",
        scratch=scratch,
    )
    for turn in range(2, ITERS):
        odd, even = exchange(message)
        rows = gather_rows(row)
        row, message, centre, rim, res, halo, direction, image, image_halo, sol, scal = call(
            functools.partial(step_kernel, count, False),
            (rows, even, odd, even_c, odd_c, centre, rim, res, halo, direction, image, image_halo,
             sol, scal, inv, blk) + shared,
            state,
            "apply%d" % turn,
            scratch=scratch,
        )
    odd, even = exchange(message)
    rows = gather_rows(row)
    sol, res = call(
        last_kernel,
        (rows, even, odd, centre, res, direction, image, sol, scal, inv, blk, cond_weight, coil),
        [tile, tile],
        "finish",
    )
    return sol, res


def solution(mesh):
    return jax.shard_map(
        functools.partial(body, mesh.shape["dom"]),
        mesh=mesh,
        in_specs=(
            P(None, "dom"),
            P(None, "dom"),
            P(None, "dom"),
            P(None, None, None, "dom"),
            P(None, "dom"),
            P(None, "dom"),
            P("dom"),
            P("dom", None),
            P(),
            P(),
            P(),
        ),
        out_specs=(P(None, "dom"), P(None, "dom")),
        check_vma=False,
    )
```

```python
import functools

import jax
import jax.numpy as jnp
from jax import lax
from jax.experimental import pallas as pl
from jax.experimental.pallas import tpu as pltpu
from jax.sharding import PartitionSpec as P

ITERS = 3
LINK_SCALE = 16.0
LANES = 128
F32 = jnp.float32
BF16 = jnp.bfloat16
VMEM = pltpu.VMEM


def gather_lanes(x, idx):
    dims = lax.GatherDimensionNumbers(
        offset_dims=(),
        collapsed_slice_dims=(1,),
        start_index_map=(1,),
        operand_batching_dims=(0,),
        start_indices_batching_dims=(0,),
    )
    return lax.gather(
        x,
        idx[..., None],
        dims,
        slice_sizes=(1, 1),
        mode=lax.GatherScatterMode.PROMISE_IN_BOUNDS,
    )


def lane_iota(rows=1, lanes=LANES):
    return lax.broadcasted_iota(jnp.int32, (rows, lanes), 1)


def nt_dot(a, b):
    return lax.dot_general(a, b, (((1,), (1,)), ((), ())), preferred_element_type=F32)


def split_rows(x):
    high = x.astype(BF16)
    low = (x - high.astype(F32)).astype(BF16)
    return jnp.concatenate([high, low], axis=0)


def add_halves(x):
    half = x.shape[0] // 2
    return x[:half] + x[half:]


def rows_of(ids):
    return jnp.concatenate([ids[i : i + 1] for i in range(ids.shape[0])], axis=1)


def onehot(ids, count):
    slots = lax.broadcasted_iota(jnp.int32, (count, ids.shape[1]), 0)
    return jnp.where(slots == ids, 1.0, 0.0).astype(BF16)


def weighted(weight, table, coils):
    parts = []
    wide = jnp.broadcast_to(table, (8, LANES))
    for i in range(coils.shape[1] // LANES):
        tile = coils[:, i * LANES : (i + 1) * LANES]
        got = gather_lanes(wide, jnp.broadcast_to(tile, (8, LANES)))
        cut = weight[:, i * LANES : (i + 1) * LANES]
        parts.append(cut * jnp.broadcast_to(got[0:1], cut.shape))
    return jnp.concatenate(parts, axis=1)


def pad_lanes(row, scratch):
    scratch[...] = jnp.zeros_like(scratch)
    scratch[0:1, 0 : row.shape[1]] = row
    return scratch[0:1, :]


def move(pairs, sems):
    copies = [pltpu.make_async_copy(src, dst, sems.at[i]) for i, (src, dst) in enumerate(pairs)]
    for copy in copies:
        copy.start()
    return copies


def rhs_kernel(
    side_hbm, weight_hbm, block_hbm, coil_hbm, phase_hbm, ohm_hbm, state_hbm, curl_hbm,
    rhs_ref, weight_ref, block_ref, coil_ref, curl_ref,
    side_ref, phase_ref, ohm_ref, state_ref, pad_ref, sems,
):
    copies = move(
        [
            (coil_hbm, coil_ref),
            (phase_hbm, phase_ref),
            (ohm_hbm, ohm_ref),
            (state_hbm, state_ref),
            (weight_hbm, weight_ref),
            (block_hbm, block_ref),
            (side_hbm, side_ref),
            (curl_hbm.at[0 : curl_ref.shape[0]], curl_ref),
        ],
        sems,
    )
    for copy in copies[:-1]:
        copy.wait()
    s0, s1, s2 = (state_ref[i].astype(F32) for i in range(3))
    mean = (s0 + s1 + s2) / 3.0
    phase = phase_ref[...]
    volts = jnp.where(
        phase == 0,
        s0 - mean,
        jnp.where(phase == 1, s1 - mean, jnp.where(phase == 2, s2 - mean, 0.0)),
    )
    source = pad_lanes(LINK_SCALE * volts / ohm_ref[...], pad_ref)
    coils, blocks = rows_of(coil_ref[...]), rows_of(block_ref[...])
    spread = split_rows(weighted(weight_ref[...], source, coils))
    rhs_ref[...] = side_ref[...] + add_halves(nt_dot(spread, onehot(blocks, LANES)))
    copies[-1].wait()


def table_kernel(
    pattern_hbm, ohm_hbm, sigma_hbm, reluct_hbm, curl_hbm, block_ref, coil_ref,
    pat_ref, blk_ref, coil_hot_ref, inv_ref, pattern_ref, sigma_ref, reluct_ref, curl_ref,
    ohm_ref, sems,
):
    copies = move(
        [
            (pattern_hbm, pattern_ref),
            (ohm_hbm, ohm_ref),
            (sigma_hbm, sigma_ref),
            (reluct_hbm, reluct_ref),
            (curl_hbm.at[2 : 2 + curl_ref.shape[0]], curl_ref),
        ],
        sems,
    )
    blk_ref[...] = onehot(rows_of(block_ref[...]), LANES)
    coil_hot_ref[...] = onehot(rows_of(coil_ref[...]), LANES)
    for copy in copies[:-1]:
        copy.wait()
    for k in range(pattern_ref.shape[0]):
        q = pattern_ref[k : k + 1, :]
        slot = jnp.where(q < 32, q + 128, jnp.where(q < 160, q - 32, q))
        pat_ref[:, k * LANES : (k + 1) * LANES] = onehot(slot, 2 * LANES)
    inv_ref[...] = jnp.zeros_like(inv_ref)
    inv_ref[0:1, 0 : ohm_ref.shape[1]] = 1.0 / ohm_ref[...]
    copies[-1].wait()


def sides(a, b):
    even = lax.rem(lax.axis_index("dom"), 2) == 0
    return jnp.where(even, b, a), jnp.where(even, a, b)


def halo_mask(count):
    me = lax.axis_index("dom")
    lane = lane_iota()
    left = jnp.where(me > 0, 1.0, 0.0)
    right = jnp.where(me < count - 1, 1.0, 0.0)
    return jnp.where(lane < 32, left, jnp.where(lane < 64, right, 0.0))


def halo_of(left, right, count):
    lane = lane_iota(*left.shape)
    moved = jnp.where(lane < 32, pltpu.roll(left, 32, 1), pltpu.roll(right, 32, 1))
    return moved * halo_mask(count)


def face_part(curl_refs, first_kind, picked_ref, first, total):
    kind = first_kind
    for curl_ref in curl_refs:
        for k in range(curl_ref.shape[0]):
            for t in range(0, picked_ref.shape[1], 8):
                term = curl_ref[k, pl.ds(first, 8), t : t + 8, :] * picked_ref[kind, t : t + 8, :][None]
                total = term if total is None else total + term
            kind += 1
    return total


def apply_local(refs, own, halo, previous, row_out, msg_out, centre_out, rim_out, scratch, late=None):
    (sigma_ref, reluct_ref, curl_refs, pattern_ref, weight_ref, block_ref, coil_ref,
     pat_ref, coil_hot_ref) = refs
    picked_ref, face_ref, back_ref, partial_ref = scratch
    width = own.shape[0]
    rows = curl_refs[0].shape[1]
    kinds = pattern_ref.shape[0]

    for k in range(kinds):
        q = pattern_ref[k : k + 1, :]
        inside = jnp.logical_and(q >= 32, q < 160)
        idx = jnp.where(q < 32, q, jnp.where(inside, q - 32, q - 128))
        idx = jnp.broadcast_to(idx, (width, LANES))
        inside = jnp.broadcast_to(inside, (width, LANES))
        picked_ref[k] = jnp.where(inside, gather_lanes(own, idx), gather_lanes(halo, idx))

    if late is not None:

        @pl.loop(0, rows // 8)
        def _(step):
            first = pl.multiple_of(step * 8, 8)
            partial_ref[pl.ds(first, 8)] = face_part(curl_refs[:2], 0, picked_ref, first, None)

        late.wait()

    @pl.loop(0, rows // 8)
    def _(step):
        first = pl.multiple_of(step * 8, 8)
        if late is None:
            total = face_part(curl_refs, 0, picked_ref, first, None)
        else:
            total = face_part(curl_refs[2:], 4, picked_ref, first, partial_ref[pl.ds(first, 8)])
        face_ref[pl.ds(first, 8), :] = jnp.sum(total, axis=1)

    face = face_ref[...]
    bent = reluct_ref[...] * face
    energy = jnp.sum(bent * face + sigma_ref[...] * own * own, axis=0, keepdims=True)
    face_ref[...] = bent

    for at, curl_ref in enumerate(curl_refs):

        @pl.loop(0, curl_ref.shape[0])
        def _(k):
            total = curl_ref[k, 0] * face_ref[0:1, :]
            for a in range(1, rows):
                total = total + curl_ref[k, a] * face_ref[a : a + 1, :]
            where = pl.multiple_of((k + 2 * at) * LANES, LANES)
            back_ref[:, pl.ds(where, LANES)] = split_rows(total)

    spread = add_halves(nt_dot(back_ref[...], pat_ref[...]))
    rim = spread[:, LANES:]
    centre = sigma_ref[...] * own + spread[:, :LANES]
    centre_out[...] = centre
    rim_out[...] = rim
    lane = lane_iota(width)
    edges = jnp.logical_or(lane < 32, lane >= 96)
    msg_out[0:width, 0:LANES] = jnp.where(
        edges, centre, jnp.where(lane < 64, rim, pltpu.roll(rim, 64, 1))
    )

    links = []
    for i in range(block_ref.shape[0]):
        idx = jnp.broadcast_to(block_ref[i : i + 1, :], (width, LANES))
        got = gather_lanes(own, idx) * weight_ref[:, i * LANES : (i + 1) * LANES]
        links.append(jnp.sum(got, axis=0, keepdims=True))
    link = jnp.concatenate(links, axis=1)
    high = link.astype(BF16).astype(F32)
    mid = (link - high).astype(BF16).astype(F32)
    low = link - high - mid
    sub = lax.broadcasted_iota(jnp.int32, (8, link.shape[1]), 0)
    terms = jnp.where(sub == 0, high, jnp.where(sub == 1, mid, jnp.where(sub == 2, low, 0.0)))
    linkage = jnp.sum(nt_dot(terms.astype(BF16), coil_hot_ref[...]), axis=0, keepdims=True)

    coils = 84
    lane = lane_iota()
    norm = jnp.sum(jnp.sum(own * own, axis=0, keepdims=True), axis=1, keepdims=True)
    energy = jnp.sum(energy, axis=1, keepdims=True)
    line = linkage + jnp.where(lane == coils, norm, 0.0) + jnp.where(lane == coils + 1, energy, 0.0)
    if previous is not None:
        msg_out[:, LANES:] = jnp.zeros_like(msg_out[:, LANES:])
        cross = jnp.sum(jnp.sum(own * previous, axis=0, keepdims=True), axis=1, keepdims=True)
        line = line + jnp.where(lane == coils + 2, cross, 0.0)
    row_out[...] = jnp.broadcast_to(line, row_out.shape)


def pick(line, at):
    return jnp.sum(jnp.where(lane_iota() == at, line, 0.0), axis=1, keepdims=True)


def first_kernel(count, rhs_ref, even_ref, odd_ref, curl_hbm, sigma_ref, reluct_ref, curl0_ref,
                 curl1_ref, pattern_ref, weight_ref, block_ref, coil_ref, pat_ref, coil_hot_ref,
                 row_ref, msg_ref, centre_ref, rim_ref, halo_ref, curl2_ref, *scratch):
    late = pltpu.make_async_copy(curl_hbm.at[4:], curl2_ref, scratch[-1])
    late.start()
    left, right = sides(even_ref[...], odd_ref[...])
    halo = halo_of(left, right, count)
    halo_ref[...] = halo
    width = rhs_ref.shape[0]
    msg_ref[0:width, LANES:] = weight_ref[...]
    msg_ref[width:, :] = jnp.zeros_like(msg_ref[width:, :])
    msg_ref[width : width + 1, LANES:] = rows_of(block_ref[...]).astype(F32)
    msg_ref[width + 1 : width + 2, LANES:] = rows_of(coil_ref[...]).astype(F32)
    refs = (sigma_ref, reluct_ref, (curl0_ref, curl1_ref, curl2_ref), pattern_ref, weight_ref,
            block_ref, coil_ref, pat_ref, coil_hot_ref)
    apply_local(refs, rhs_ref[...], halo, None, row_ref, msg_ref, centre_ref, rim_ref, scratch[:-1],
                late)


def scalars(rows_ref, inv_ref, scal_ref):
    coils = 84
    total = jnp.sum(rows_ref[...], axis=0, keepdims=True)
    current = total * inv_ref[0:1, :]
    norm, energy = pick(total, coils), pick(total, coils + 1)
    energy = energy + jnp.sum(current * total, axis=1, keepdims=True)
    if scal_ref is None:
        beta = None
        curve = energy
    else:
        beta = norm / pick(scal_ref[0:1, :], 0)
        cross = pick(total, coils + 2)
        curve = energy + 2.0 * beta * cross + beta * beta * pick(scal_ref[0:1, :], 1)
    lane = lane_iota()
    state = jnp.where(lane == 0, norm, jnp.where(lane == 1, curve, 0.0))
    return current, norm / curve, beta, state


def own_image(left, right, centre, weight, current, coils, blk):
    lane = lane_iota(*centre.shape)
    image = centre + jnp.where(lane < 32, pltpu.roll(left, 96, 1), 0.0)
    image = image + jnp.where(lane >= 96, pltpu.roll(right, 32, 1), 0.0)
    return image + add_halves(nt_dot(split_rows(weighted(weight, current, coils)), blk))


def step_kernel(count, first, *refs):
    names = ["rows", "even", "odd"] + ([] if first else ["evenc", "oddc"])
    names += ["centre", "rim", "res", "halo"] + ([] if first else ["dir", "img", "imgh", "sol", "scal"])
    names += ["inv", "blk", "sigma", "reluct", "curl0", "curl1", "curl2", "pattern", "weight",
              "block", "coil", "pat", "coilhot"]
    names += ["row_o", "msg_o", "centre_o", "rim_o", "res_o", "halo_o", "dir_o", "img_o", "imgh_o",
              "sol_o", "scal_o"]
    r = dict(zip(names, refs))
    scratch = refs[len(names):]
    width = r["res"].shape[0]
    current, alpha, beta, state = scalars(r["rows"], r["inv"], r.get("scal"))
    r["scal_o"][...] = jnp.broadcast_to(state, r["scal_o"].shape)

    left, right = sides(r["even"][0:width, 0:LANES], r["odd"][0:width, 0:LANES])
    image = own_image(left, right, r["centre"][...], r["weight"][...], current,
                      rows_of(r["coil"][...]), r["blk"][...])

    ce, co = (r["even"], r["odd"]) if first else (r["evenc"], r["oddc"])
    cl, cr = sides(ce[:, LANES:], co[:, LANES:])
    spot = jnp.concatenate(
        [cl[width : width + 1].astype(jnp.int32) - 96, cr[width : width + 1].astype(jnp.int32) + 32],
        axis=1,
    )
    amount = jnp.concatenate(
        [
            weighted(c[0:width], current, c[width + 1 : width + 2].astype(jnp.int32))
            for c in (cl, cr)
        ],
        axis=1,
    )
    beyond = add_halves(nt_dot(split_rows(amount), onehot(spot, LANES)))
    lane = lane_iota(width)
    moved = jnp.where(lane < 32, pltpu.roll(left, 32, 1), pltpu.roll(right, 32, 1))
    image_halo = (moved + r["rim"][...] + beyond) * halo_mask(count)

    old = r["res"][...]
    if first:
        direction = old
        r["sol_o"][...] = alpha * direction
    else:
        direction = old + beta * r["dir"][...]
        image = image + beta * r["img"][...]
        image_halo = image_halo + beta * r["imgh"][...]
        r["sol_o"][...] = r["sol"][...] + alpha * direction
    r["dir_o"][...] = direction
    r["img_o"][...] = image
    r["imgh_o"][...] = image_halo
    own = old - alpha * image
    halo = r["halo"][...] - alpha * image_halo
    r["res_o"][...] = own
    r["halo_o"][...] = halo
    refs = (r["sigma"], r["reluct"], (r["curl0"], r["curl1"], r["curl2"]))
    refs += tuple(r[k] for k in ("pattern", "weight", "block", "coil", "pat", "coilhot"))
    apply_local(refs, own, halo, image, r["row_o"], r["msg_o"], r["centre_o"], r["rim_o"], scratch)


def last_kernel(rows_ref, even_ref, odd_ref, centre_ref, res_ref, dir_ref, img_ref, sol_ref, scal_ref,
                inv_ref, blk_ref, weight_ref, coil_ref, sol_out, res_out):
    current, alpha, beta, _ = scalars(rows_ref, inv_ref, scal_ref)
    left, right = sides(even_ref[:, 0:LANES], odd_ref[:, 0:LANES])
    image = own_image(left, right, centre_ref[...], weight_ref[...], current,
                      rows_of(coil_ref[...]), blk_ref[...])
    image = image + beta * img_ref[...]
    sol_out[...] = sol_ref[...] + alpha * (res_ref[...] + beta * dir_ref[...])
    res_out[...] = res_ref[...] - alpha * image


def call(kernel, args, outs, name, hbm=(), scratch=()):
    args = [
        pltpu.with_memory_space_constraint(x, pltpu.HBM) if i in hbm else x
        for i, x in enumerate(args)
    ]
    return pl.pallas_call(
        kernel,
        name=name,
        in_specs=[
            pl.BlockSpec(memory_space=pltpu.HBM if i in hbm else VMEM) for i in range(len(args))
        ],
        out_specs=[pl.BlockSpec(memory_space=VMEM)] * len(outs),
        out_shape=[jax.ShapeDtypeStruct(s, d) for s, d in outs],
        scratch_shapes=list(scratch),
        compiler_params=pltpu.CompilerParams(vmem_limit_bytes=8 << 20),
    )(*args)


def body(count, right_side, sigma, reluctivity, curl_blocks, pattern, cond_weight, cond_block,
         cond_coil, coil_phase, coil_resistance, switch_state):
    width, blocks = right_side.shape
    kinds = pattern.shape[0]
    conductors = cond_weight.shape[1]
    block = cond_block.reshape(-1, LANES)
    coil = cond_coil.reshape(-1, LANES)
    phase = coil_phase.reshape(1, -1)
    ohm = coil_resistance.reshape(1, -1)
    tile = ((width, LANES), F32)

    inner = [(i, i ^ 1) for i in range(count)]
    outer = [(i, i + 1) for i in range(1, count - 1, 2)]
    outer = outer + [(b, a) for a, b in outer]

    def exchange(message):
        return lax.ppermute(message, "dom", outer), lax.ppermute(message, "dom", inner)

    def gather_rows(rows):
        return lax.all_to_all(rows, "dom", 0, 0, tiled=True)

    def like(x, count=None):
        return ((x.shape if count is None else (count,) + x.shape[1:]), x.dtype)

    rhs, weight_v, block_v, coil_v, curl0 = call(
        rhs_kernel,
        (right_side, cond_weight, block, coil, phase, ohm, switch_state, curl_blocks),
        [tile, like(cond_weight), like(block), like(coil), like(curl_blocks, 2)],
        "rhs",
        hbm=range(8),
        scratch=[VMEM((width, LANES), F32), VMEM(phase.shape, phase.dtype), VMEM(ohm.shape, F32),
                 pltpu.SMEM(switch_state.shape, switch_state.dtype), VMEM((8, LANES), F32),
                 pltpu.SemaphoreType.DMA((8,))],
    )
    odd, even = exchange(rhs)
    pat, blk, coil_hot, inv, pattern_v, sigma_v, reluct_v, curl1 = call(
        table_kernel,
        (pattern, ohm, sigma, reluctivity, curl_blocks, block_v, coil_v),
        [((2 * LANES, kinds * LANES), BF16), ((LANES, conductors), BF16),
         ((LANES, conductors), BF16), ((8, LANES), F32), like(pattern), tile, tile,
         like(curl_blocks, 2)],
        "tables",
        hbm=range(5),
        scratch=[VMEM(ohm.shape, F32), pltpu.SemaphoreType.DMA((5,))],
    )
    scratch = [VMEM((kinds, width, LANES), F32), VMEM((width, LANES), F32),
               VMEM((2 * width, kinds * LANES), BF16), VMEM((width, 8, LANES), F32)]
    plane = (pattern_v, weight_v, block_v, coil_v, pat, coil_hot)
    line = ((count, LANES), F32)
    wide = ((width + 8, LANES + conductors), F32)
    row, message, centre, rim, halo, curl2 = call(
        functools.partial(first_kernel, count),
        (rhs, even, odd, curl_blocks, sigma_v, reluct_v, curl0, curl1) + plane,
        [line, wide, tile, tile, tile, like(curl_blocks, 2)],
        "apply0",
        hbm=(3,),
        scratch=scratch + [pltpu.SemaphoreType.DMA(())],
    )
    shared = (sigma_v, reluct_v, curl0, curl1, curl2) + plane
    odd_c, even_c = odd, even = exchange(message)
    rows = gather_rows(row)
    state = [line, ((width, 3 * LANES), F32), tile, tile, tile, tile, tile, tile, tile, tile, ((8, LANES), F32)]
    row, message, centre, rim, res, halo, direction, image, image_halo, sol, scal = call(
        functools.partial(step_kernel, count, True),
        (rows, even, odd, centre, rim, rhs, halo, inv, blk) + shared,
        state,
        "apply1",
        scratch=scratch,
    )
    for turn in range(2, ITERS):
        odd, even = exchange(message)
        rows = gather_rows(row)
        row, message, centre, rim, res, halo, direction, image, image_halo, sol, scal = call(
            functools.partial(step_kernel, count, False),
            (rows, even, odd, even_c, odd_c, centre, rim, res, halo, direction, image, image_halo,
             sol, scal, inv, blk) + shared,
            state,
            "apply%d" % turn,
            scratch=scratch,
        )
    odd, even = exchange(message)
    rows = gather_rows(row)
    sol, res = call(
        last_kernel,
        (rows, even, odd, centre, res, direction, image, sol, scal, inv, blk, weight_v, coil_v),
        [tile, tile],
        "finish",
    )
    return sol, res


def solution(mesh):
    return jax.shard_map(
        functools.partial(body, mesh.shape["dom"]),
        mesh=mesh,
        in_specs=(
            P(None, "dom"),
            P(None, "dom"),
            P(None, "dom"),
            P(None, None, None, "dom"),
            P(None, "dom"),
            P(None, "dom"),
            P("dom"),
            P("dom", None),
            P(),
            P(),
            P(),
        ),
        out_specs=(P(None, "dom"), P(None, "dom")),
        check_vma=False,
    )
```

```python
import functools

import jax
import jax.numpy as jnp
from jax import lax
from jax.experimental import pallas as pl
from jax.experimental.pallas import tpu as pltpu
from jax.sharding import PartitionSpec as P

ITERS = 3
LINK_SCALE = 16.0
LANES = 128
COILS = 84
COST = 1 << 34
F32 = jnp.float32
BF16 = jnp.bfloat16
VMEM = pltpu.VMEM


def gather_lanes(x, idx):
    dims = lax.GatherDimensionNumbers(
        offset_dims=(),
        collapsed_slice_dims=(1,),
        start_index_map=(1,),
        operand_batching_dims=(0,),
        start_indices_batching_dims=(0,),
    )
    return lax.gather(
        x,
        idx[..., None],
        dims,
        slice_sizes=(1, 1),
        mode=lax.GatherScatterMode.PROMISE_IN_BOUNDS,
    )


def lane_iota(rows=1, lanes=LANES):
    return lax.broadcasted_iota(jnp.int32, (rows, lanes), 1)


def nt_dot(a, b):
    return lax.dot_general(a, b, (((1,), (1,)), ((), ())), preferred_element_type=F32)


def split_rows(x):
    high = x.astype(BF16)
    low = (x - high.astype(F32)).astype(BF16)
    return jnp.concatenate([high, low], axis=0)


def add_halves(x):
    half = x.shape[0] // 2
    return x[:half] + x[half:]


def rows_of(ids):
    return jnp.concatenate([ids[i : i + 1] for i in range(ids.shape[0])], axis=1)


def onehot(ids, count):
    slots = lax.broadcasted_iota(jnp.int32, (count, ids.shape[1]), 0)
    return jnp.where(slots == ids, 1.0, 0.0).astype(BF16)


def weighted(weight, table, coils):
    parts = []
    wide = jnp.broadcast_to(table, (8, LANES))
    for i in range(coils.shape[1] // LANES):
        tile = coils[:, i * LANES : (i + 1) * LANES]
        got = gather_lanes(wide, jnp.broadcast_to(tile, (8, LANES)))
        cut = weight[:, i * LANES : (i + 1) * LANES]
        parts.append(cut * jnp.broadcast_to(got[0:1], cut.shape))
    return jnp.concatenate(parts, axis=1)


def pad_lanes(row, scratch):
    scratch[...] = jnp.zeros_like(scratch)
    scratch[0:1, 0 : row.shape[1]] = row
    return scratch[0:1, :]


def move(pairs, sems):
    copies = [pltpu.make_async_copy(src, dst, sems.at[i]) for i, (src, dst) in enumerate(pairs)]
    for copy in copies:
        copy.start()
    return copies


def rhs_kernel(
    side_hbm, weight_hbm, block_hbm, coil_hbm, phase_hbm, ohm_hbm, state_hbm,
    rhs_ref, weight_ref, block_ref, coil_ref,
    side_ref, phase_ref, ohm_ref, state_ref, pad_ref, sems,
):
    copies = move(
        [
            (coil_hbm, coil_ref),
            (phase_hbm, phase_ref),
            (ohm_hbm, ohm_ref),
            (state_hbm, state_ref),
            (weight_hbm, weight_ref),
            (block_hbm, block_ref),
            (side_hbm, side_ref),
        ],
        sems,
    )
    for copy in copies:
        copy.wait()
    s0, s1, s2 = (state_ref[i].astype(F32) for i in range(3))
    mean = (s0 + s1 + s2) / 3.0
    phase = phase_ref[...]
    volts = jnp.where(
        phase == 0,
        s0 - mean,
        jnp.where(phase == 1, s1 - mean, jnp.where(phase == 2, s2 - mean, 0.0)),
    )
    source = pad_lanes(LINK_SCALE * volts / ohm_ref[...], pad_ref)
    coils, blocks = rows_of(coil_ref[...]), rows_of(block_ref[...])
    spread = split_rows(weighted(weight_ref[...], source, coils))
    rhs_ref[...] = side_ref[...] + add_halves(nt_dot(spread, onehot(blocks, LANES)))


def table_kernel(
    pattern_hbm, ohm_hbm, sigma_hbm, reluct_hbm, block_ref, coil_ref,
    pat_ref, blk_ref, coil_hot_ref, inv_ref, pattern_ref, sigma_ref, reluct_ref,
    ohm_ref, sems,
):
    copies = move(
        [
            (pattern_hbm, pattern_ref),
            (ohm_hbm, ohm_ref),
            (sigma_hbm, sigma_ref),
            (reluct_hbm, reluct_ref),
        ],
        sems,
    )
    blk_ref[...] = onehot(rows_of(block_ref[...]), LANES)
    coil_hot_ref[...] = onehot(rows_of(coil_ref[...]), LANES)
    for copy in copies:
        copy.wait()
    for k in range(pattern_ref.shape[0]):
        q = pattern_ref[k : k + 1, :]
        slot = jnp.where(q < 32, q + 128, jnp.where(q < 160, q - 32, q))
        pat_ref[:, k * LANES : (k + 1) * LANES] = onehot(slot, 2 * LANES)
    inv_ref[...] = jnp.zeros_like(inv_ref)
    inv_ref[0:1, 0 : ohm_ref.shape[1]] = 1.0 / ohm_ref[...]


def sides(a, b):
    even = lax.rem(lax.axis_index("dom"), 2) == 0
    return jnp.where(even, b, a), jnp.where(even, a, b)


def halo_mask(count):
    me = lax.axis_index("dom")
    lane = lane_iota()
    left = jnp.where(me > 0, 1.0, 0.0)
    right = jnp.where(me < count - 1, 1.0, 0.0)
    return jnp.where(lane < 32, left, jnp.where(lane < 64, right, 0.0))


def halo_of(left, right, count):
    lane = lane_iota(*left.shape)
    moved = jnp.where(lane < 32, pltpu.roll(left, 32, 1), pltpu.roll(right, 32, 1))
    return moved * halo_mask(count)


def pick_edges(pattern_ref, own, halo, picked_ref):
    width = own.shape[0]
    for k in range(pattern_ref.shape[0]):
        q = pattern_ref[k : k + 1, :]
        inside = jnp.logical_and(q >= 32, q < 160)
        idx = jnp.where(q < 32, q, jnp.where(inside, q - 32, q - 128))
        idx = jnp.broadcast_to(idx, (width, LANES))
        inside = jnp.broadcast_to(inside, (width, LANES))
        picked_ref[k] = jnp.where(inside, gather_lanes(own, idx), gather_lanes(halo, idx))


def forward(curl_ref, picked_ref, face_ref):
    kinds, rows, width, _ = curl_ref.shape

    @pl.loop(0, rows // 8)
    def _(step):
        first = pl.multiple_of(step * 8, 8)
        total = None
        for k in range(kinds):
            for t in range(0, width, 8):
                term = curl_ref[k, pl.ds(first, 8), t : t + 8, :] * picked_ref[k, t : t + 8, :][None]
                total = term if total is None else total + term
        face_ref[pl.ds(first, 8), :] = jnp.sum(total, axis=1)


def backward(curl_ref, bent_ref, back_ref, pat_ref, sigma_ref, own, centre_out, rim_out, msg_out):
    kinds, rows, width, _ = curl_ref.shape

    @pl.loop(0, kinds)
    def _(k):
        total = curl_ref[k, 0] * bent_ref[0:1, :]
        for a in range(1, rows):
            total = total + curl_ref[k, a] * bent_ref[a : a + 1, :]
        back_ref[:, pl.ds(pl.multiple_of(k * LANES, LANES), LANES)] = split_rows(total)

    spread = add_halves(nt_dot(back_ref[...], pat_ref[...]))
    rim = spread[:, LANES:]
    centre = sigma_ref[...] * own + spread[:, :LANES]
    centre_out[...] = centre
    if rim_out is not None:
        rim_out[...] = rim
    lane = lane_iota(width)
    edges = jnp.logical_or(lane < 32, lane >= 96)
    msg_out[0:width, 0:LANES] = jnp.where(
        edges, centre, jnp.where(lane < 64, rim, pltpu.roll(rim, 64, 1))
    )


def summed_row(own, previous, energy, weight_ref, block_ref, coil_hot_ref, row_out):
    width = own.shape[0]
    links = []
    for i in range(block_ref.shape[0]):
        idx = jnp.broadcast_to(block_ref[i : i + 1, :], (width, LANES))
        got = gather_lanes(own, idx) * weight_ref[:, i * LANES : (i + 1) * LANES]
        links.append(jnp.sum(got, axis=0, keepdims=True))
    link = jnp.concatenate(links, axis=1)
    high = link.astype(BF16).astype(F32)
    mid = (link - high).astype(BF16).astype(F32)
    low = link - high - mid
    sub = lax.broadcasted_iota(jnp.int32, (8, link.shape[1]), 0)
    terms = jnp.where(sub == 0, high, jnp.where(sub == 1, mid, jnp.where(sub == 2, low, 0.0)))
    linkage = jnp.sum(nt_dot(terms.astype(BF16), coil_hot_ref[...]), axis=0, keepdims=True)

    lane = lane_iota()
    norm = jnp.sum(jnp.sum(own * own, axis=0, keepdims=True), axis=1, keepdims=True)
    energy = jnp.sum(energy, axis=1, keepdims=True)
    line = linkage + jnp.where(lane == COILS, norm, 0.0) + jnp.where(lane == COILS + 1, energy, 0.0)
    if previous is not None:
        cross = jnp.sum(jnp.sum(own * previous, axis=0, keepdims=True), axis=1, keepdims=True)
        line = line + jnp.where(lane == COILS + 2, cross, 0.0)
    row_out[...] = jnp.broadcast_to(line, row_out.shape)


def face_side(refs, own, halo, previous, row_out, picked_ref, face_ref):
    sigma_ref, reluct_ref, curl_ref, pattern_ref, weight_ref, block_ref, coil_hot_ref = refs
    pick_edges(pattern_ref, own, halo, picked_ref)
    forward(curl_ref, picked_ref, face_ref)
    face = face_ref[...]
    bent = reluct_ref[...] * face
    face_ref[...] = bent
    energy = jnp.sum(bent * face + sigma_ref[...] * own * own, axis=0, keepdims=True)
    summed_row(own, previous, energy, weight_ref, block_ref, coil_hot_ref, row_out)


def pick(line, at):
    return jnp.sum(jnp.where(lane_iota() == at, line, 0.0), axis=1, keepdims=True)


def first_kernel(count, rhs_ref, even_ref, odd_ref, sigma_ref, reluct_ref, curl_ref, pattern_ref,
                 weight_ref, block_ref, coil_hot_ref, pat_ref, coil_ref,
                 row_ref, msg_ref, centre_ref, rim_ref, halo_ref,
                 picked_ref, face_ref, back_ref):
    left, right = sides(even_ref[...], odd_ref[...])
    halo = halo_of(left, right, count)
    halo_ref[...] = halo
    width = rhs_ref.shape[0]
    msg_ref[0:width, LANES:] = weight_ref[...]
    msg_ref[width:, :] = jnp.zeros_like(msg_ref[width:, :])
    msg_ref[width : width + 1, LANES:] = rows_of(block_ref[...]).astype(F32)
    msg_ref[width + 1 : width + 2, LANES:] = rows_of(coil_ref[...]).astype(F32)
    own = rhs_ref[...]
    refs = (sigma_ref, reluct_ref, curl_ref, pattern_ref, weight_ref, block_ref, coil_hot_ref)
    face_side(refs, own, halo, None, row_ref, picked_ref, face_ref)
    backward(curl_ref, face_ref, back_ref, pat_ref, sigma_ref, own, centre_ref, rim_ref, msg_ref)


def scalars(rows_ref, inv_ref, scal_ref):
    total = jnp.sum(rows_ref[...], axis=0, keepdims=True)
    current = total * inv_ref[0:1, :]
    norm, energy = pick(total, COILS), pick(total, COILS + 1)
    energy = energy + jnp.sum(current * total, axis=1, keepdims=True)
    if scal_ref is None:
        beta = None
        curve = energy
    else:
        beta = norm / pick(scal_ref[0:1, :], 0)
        cross = pick(total, COILS + 2)
        curve = energy + 2.0 * beta * cross + beta * beta * pick(scal_ref[0:1, :], 1)
    lane = lane_iota()
    state = jnp.where(lane == 0, norm, jnp.where(lane == 1, curve, 0.0))
    return current, norm / curve, beta, state


def own_image(left, right, centre, weight, current, coils, blk):
    lane = lane_iota(*centre.shape)
    image = centre + jnp.where(lane < 32, pltpu.roll(left, 96, 1), 0.0)
    image = image + jnp.where(lane >= 96, pltpu.roll(right, 32, 1), 0.0)
    return image + add_halves(nt_dot(split_rows(weighted(weight, current, coils)), blk))


def step_kernel(count, first, last, *refs):
    names = ["rows", "even", "odd"] + ([] if first else ["evenc", "oddc"])
    names += ["centre", "rim", "res", "halo"] + ([] if first else ["dir", "img", "imgh", "sol", "scal"])
    names += ["inv", "blk", "sigma", "reluct", "curl", "pattern", "weight", "block", "coilhot", "pat",
              "coil"]
    names += ["row_o", "res_o", "dir_o", "img_o", "sol_o", "scal_o"]
    names += ["msg_o", "centre_o"] + ([] if last else ["rim_o", "halo_o", "imgh_o"])
    r = dict(zip(names, refs))
    scratch = refs[len(names):]
    width = r["res"].shape[0]
    current, alpha, beta, state = scalars(r["rows"], r["inv"], r.get("scal"))
    r["scal_o"][...] = jnp.broadcast_to(state, r["scal_o"].shape)

    left, right = sides(r["even"][0:width, 0:LANES], r["odd"][0:width, 0:LANES])
    image = own_image(left, right, r["centre"][...], r["weight"][...], current,
                      rows_of(r["coil"][...]), r["blk"][...])

    ce, co = (r["even"], r["odd"]) if first else (r["evenc"], r["oddc"])
    cl, cr = sides(ce[:, LANES:], co[:, LANES:])
    spot = jnp.concatenate(
        [cl[width : width + 1].astype(jnp.int32) - 96, cr[width : width + 1].astype(jnp.int32) + 32],
        axis=1,
    )
    amount = jnp.concatenate(
        [
            weighted(c[0:width], current, c[width + 1 : width + 2].astype(jnp.int32))
            for c in (cl, cr)
        ],
        axis=1,
    )
    beyond = add_halves(nt_dot(split_rows(amount), onehot(spot, LANES)))
    lane = lane_iota(width)
    moved = jnp.where(lane < 32, pltpu.roll(left, 32, 1), pltpu.roll(right, 32, 1))
    image_halo = (moved + r["rim"][...] + beyond) * halo_mask(count)

    old = r["res"][...]
    if first:
        direction = old
        r["sol_o"][...] = alpha * direction
    else:
        direction = old + beta * r["dir"][...]
        image = image + beta * r["img"][...]
        image_halo = image_halo + beta * r["imgh"][...]
        r["sol_o"][...] = r["sol"][...] + alpha * direction
    r["dir_o"][...] = direction
    r["img_o"][...] = image
    own = old - alpha * image
    halo = r["halo"][...] - alpha * image_halo
    r["res_o"][...] = own
    refs = tuple(r[k] for k in ("sigma", "reluct", "curl", "pattern", "weight", "block", "coilhot"))
    picked_ref, face_ref, back_ref = scratch
    face_side(refs, own, halo, image, r["row_o"], picked_ref, face_ref)
    if not last:
        r["imgh_o"][...] = image_halo
        r["halo_o"][...] = halo
        r["msg_o"][:, LANES:] = jnp.zeros_like(r["msg_o"][:, LANES:])
    backward(r["curl"], face_ref, back_ref, r["pat"], r["sigma"], own, r["centre_o"], r.get("rim_o"),
             r["msg_o"])


def last_kernel(rows_ref, even_ref, odd_ref, centre_ref, res_ref, dir_ref, img_ref, sol_ref, scal_ref,
                inv_ref, blk_ref, weight_ref, coil_ref, sol_out, res_out):
    current, alpha, beta, _ = scalars(rows_ref, inv_ref, scal_ref)
    left, right = sides(even_ref[:, 0:LANES], odd_ref[:, 0:LANES])
    image = own_image(left, right, centre_ref[...], weight_ref[...], current,
                      rows_of(coil_ref[...]), blk_ref[...])
    image = image + beta * img_ref[...]
    sol_out[...] = sol_ref[...] + alpha * (res_ref[...] + beta * dir_ref[...])
    res_out[...] = res_ref[...] - alpha * image


def call(kernel, args, outs, name, hbm=(), scratch=(), cost=None):
    args = [
        pltpu.with_memory_space_constraint(x, pltpu.HBM) if i in hbm else x
        for i, x in enumerate(args)
    ]
    if cost is not None:
        cost = pl.CostEstimate(flops=cost, transcendentals=0, bytes_accessed=1 << 20)
    return pl.pallas_call(
        kernel,
        name=name,
        in_specs=[
            pl.BlockSpec(memory_space=pltpu.HBM if i in hbm else VMEM) for i in range(len(args))
        ],
        out_specs=[pl.BlockSpec(memory_space=VMEM)] * len(outs),
        out_shape=[jax.ShapeDtypeStruct(s, d) for s, d in outs],
        scratch_shapes=list(scratch),
        cost_estimate=cost,
        compiler_params=pltpu.CompilerParams(vmem_limit_bytes=8 << 20),
    )(*args)


def body(count, right_side, sigma, reluctivity, curl_blocks, pattern, cond_weight, cond_block,
         cond_coil, coil_phase, coil_resistance, switch_state):
    width, blocks = right_side.shape
    kinds = pattern.shape[0]
    conductors = cond_weight.shape[1]
    block = cond_block.reshape(-1, LANES)
    coil = cond_coil.reshape(-1, LANES)
    phase = coil_phase.reshape(1, -1)
    ohm = coil_resistance.reshape(1, -1)
    tile = ((width, LANES), F32)

    inner = [(i, i ^ 1) for i in range(count)]
    outer = [(i, i + 1) for i in range(1, count - 1, 2)]
    outer = outer + [(b, a) for a, b in outer]

    def exchange(message):
        return lax.ppermute(message, "dom", outer), lax.ppermute(message, "dom", inner)

    def gather_rows(rows):
        return lax.all_to_all(rows, "dom", 0, 0, tiled=True)

    def like(x):
        return (x.shape, x.dtype)

    rhs, weight_v, block_v, coil_v = call(
        rhs_kernel,
        (right_side, cond_weight, block, coil, phase, ohm, switch_state),
        [tile, like(cond_weight), like(block), like(coil)],
        "rhs",
        hbm=range(7),
        scratch=[VMEM((width, LANES), F32), VMEM(phase.shape, phase.dtype), VMEM(ohm.shape, F32),
                 pltpu.SMEM(switch_state.shape, switch_state.dtype), VMEM((8, LANES), F32),
                 pltpu.SemaphoreType.DMA((7,))],
        cost=COST,
    )
    odd, even = exchange(rhs)
    pat, blk, coil_hot, inv, pattern_v, sigma_v, reluct_v = call(
        table_kernel,
        (pattern, ohm, sigma, reluctivity, block_v, coil_v),
        [((2 * LANES, kinds * LANES), BF16), ((LANES, conductors), BF16),
         ((LANES, conductors), BF16), ((8, LANES), F32), like(pattern), tile, tile],
        "tables",
        hbm=range(4),
        scratch=[VMEM(ohm.shape, F32), pltpu.SemaphoreType.DMA((4,))],
        cost=COST,
    )
    picked, faces = VMEM((kinds, width, LANES), F32), VMEM((width, LANES), F32)
    back = VMEM((2 * width, kinds * LANES), BF16)
    shared = (sigma_v, reluct_v, curl_blocks, pattern_v, weight_v, block_v, coil_hot, pat, coil_v)
    line = ((count, LANES), F32)
    wide = ((width + 8, LANES + conductors), F32)
    row, message, centre, rim, halo = call(
        functools.partial(first_kernel, count),
        (rhs, even, odd) + shared,
        [line, wide, tile, tile, tile],
        "apply0",
        scratch=[picked, faces, back],
    )
    odd_c, even_c = odd, even = exchange(message)
    rows = gather_rows(row)
    res, direction, image, image_halo, sol, scal = rhs, None, None, None, None, None
    for turn in range(1, ITERS):
        first, last = turn == 1, turn == ITERS - 1
        args = (rows, even, odd) + (() if first else (even_c, odd_c)) + (centre, rim, res, halo)
        args += () if first else (direction, image, image_halo, sol, scal)
        state = [line, tile, tile, tile, tile, ((8, LANES), F32)]
        state += [tile] * 2 if last else [((width, 3 * LANES), F32)] + [tile] * 4
        row, res, direction, image, sol, scal, message, centre, *rest = call(
            functools.partial(step_kernel, count, first, last),
            args + (inv, blk) + shared,
            state,
            "apply%d" % turn,
            scratch=[picked, faces, back],
        )
        if not last:
            rim, halo, image_halo = rest
        odd, even = exchange(message)
        rows = gather_rows(row)
    sol, res = call(
        last_kernel,
        (rows, even, odd, centre, res, direction, image, sol, scal, inv, blk, weight_v, coil_v),
        [tile, tile],
        "finish",
    )
    return sol, res


def solution(mesh):
    return jax.shard_map(
        functools.partial(body, mesh.shape["dom"]),
        mesh=mesh,
        in_specs=(
            P(None, "dom"),
            P(None, "dom"),
            P(None, "dom"),
            P(None, None, None, "dom"),
            P(None, "dom"),
            P(None, "dom"),
            P("dom"),
            P("dom", None),
            P(),
            P(),
            P(),
        ),
        out_specs=(P(None, "dom"), P(None, "dom")),
        check_vma=False,
    )
```

```python
import functools

import jax
import jax.numpy as jnp
from jax import lax
from jax.experimental import pallas as pl
from jax.experimental.pallas import tpu as pltpu
from jax.sharding import PartitionSpec as P

ITERS = 3
LINK_SCALE = 16.0
LANES = 128
COILS = 84
COST = 1 << 34
F32 = jnp.float32
BF16 = jnp.bfloat16
VMEM = pltpu.VMEM


def gather_lanes(x, idx):
    dims = lax.GatherDimensionNumbers(
        offset_dims=(),
        collapsed_slice_dims=(1,),
        start_index_map=(1,),
        operand_batching_dims=(0,),
        start_indices_batching_dims=(0,),
    )
    return lax.gather(
        x,
        idx[..., None],
        dims,
        slice_sizes=(1, 1),
        mode=lax.GatherScatterMode.PROMISE_IN_BOUNDS,
    )


def lane_iota(rows=1, lanes=LANES):
    return lax.broadcasted_iota(jnp.int32, (rows, lanes), 1)


def nt_dot(a, b):
    return lax.dot_general(a, b, (((1,), (1,)), ((), ())), preferred_element_type=F32)


def split_rows(x):
    high = x.astype(BF16)
    low = (x - high.astype(F32)).astype(BF16)
    return jnp.concatenate([high, low], axis=0)


def add_halves(x):
    half = x.shape[0] // 2
    return x[:half] + x[half:]


def rows_of(ids):
    return jnp.concatenate([ids[i : i + 1] for i in range(ids.shape[0])], axis=1)


def onehot(ids, count):
    slots = lax.broadcasted_iota(jnp.int32, (count, ids.shape[1]), 0)
    return jnp.where(slots == ids, 1.0, 0.0).astype(BF16)


def weighted(weight, table, coils):
    parts = []
    wide = jnp.broadcast_to(table, (8, LANES))
    for i in range(coils.shape[1] // LANES):
        tile = coils[:, i * LANES : (i + 1) * LANES]
        got = gather_lanes(wide, jnp.broadcast_to(tile, (8, LANES)))
        cut = weight[:, i * LANES : (i + 1) * LANES]
        parts.append(cut * jnp.broadcast_to(got[0:1], cut.shape))
    return jnp.concatenate(parts, axis=1)


def pad_lanes(row, scratch):
    scratch[...] = jnp.zeros_like(scratch)
    scratch[0:1, 0 : row.shape[1]] = row
    return scratch[0:1, :]


def move(pairs, sems):
    copies = [pltpu.make_async_copy(src, dst, sems.at[i]) for i, (src, dst) in enumerate(pairs)]
    for copy in copies:
        copy.start()
    return copies


def rhs_kernel(
    side_hbm, weight_hbm, block_hbm, coil_hbm, phase_hbm, ohm_hbm, state_hbm,
    rhs_ref, weight_ref, block_ref, coil_ref,
    side_ref, phase_ref, ohm_ref, state_ref, pad_ref, sems,
):
    copies = move(
        [
            (coil_hbm, coil_ref),
            (phase_hbm, phase_ref),
            (ohm_hbm, ohm_ref),
            (state_hbm, state_ref),
            (weight_hbm, weight_ref),
            (block_hbm, block_ref),
            (side_hbm, side_ref),
        ],
        sems,
    )
    for copy in copies:
        copy.wait()
    s0, s1, s2 = (state_ref[i].astype(F32) for i in range(3))
    mean = (s0 + s1 + s2) / 3.0
    phase = phase_ref[...]
    volts = jnp.where(
        phase == 0,
        s0 - mean,
        jnp.where(phase == 1, s1 - mean, jnp.where(phase == 2, s2 - mean, 0.0)),
    )
    source = pad_lanes(LINK_SCALE * volts / ohm_ref[...], pad_ref)
    coils, blocks = rows_of(coil_ref[...]), rows_of(block_ref[...])
    spread = split_rows(weighted(weight_ref[...], source, coils))
    rhs_ref[...] = side_ref[...] + add_halves(nt_dot(spread, onehot(blocks, LANES)))


def table_kernel(
    pattern_hbm, ohm_hbm, sigma_hbm, reluct_hbm, block_ref, coil_ref,
    pat_ref, blk_ref, coil_hot_ref, inv_ref, pattern_ref, sigma_ref, reluct_ref,
    ohm_ref, sems,
):
    copies = move(
        [
            (pattern_hbm, pattern_ref),
            (ohm_hbm, ohm_ref),
            (sigma_hbm, sigma_ref),
            (reluct_hbm, reluct_ref),
        ],
        sems,
    )
    blk_ref[...] = onehot(rows_of(block_ref[...]), LANES)
    coil_hot_ref[...] = onehot(rows_of(coil_ref[...]), LANES)
    for copy in copies:
        copy.wait()
    for k in range(pattern_ref.shape[0]):
        q = pattern_ref[k : k + 1, :]
        slot = jnp.where(q < 32, q + 128, jnp.where(q < 160, q - 32, q))
        pat_ref[:, k * LANES : (k + 1) * LANES] = onehot(slot, 2 * LANES)
    inv_ref[...] = jnp.zeros_like(inv_ref)
    inv_ref[0:1, 0 : ohm_ref.shape[1]] = 1.0 / ohm_ref[...]


def sides(a, b):
    even = lax.rem(lax.axis_index("dom"), 2) == 0
    return jnp.where(even, b, a), jnp.where(even, a, b)


def halo_mask(count):
    me = lax.axis_index("dom")
    lane = lane_iota()
    left = jnp.where(me > 0, 1.0, 0.0)
    right = jnp.where(me < count - 1, 1.0, 0.0)
    return jnp.where(lane < 32, left, jnp.where(lane < 64, right, 0.0))


def halo_of(left, right, count):
    lane = lane_iota(*left.shape)
    moved = jnp.where(lane < 32, pltpu.roll(left, 32, 1), pltpu.roll(right, 32, 1))
    return moved * halo_mask(count)


def pick_edges(pattern_ref, own, halo, picked_ref):
    width = own.shape[0]
    for k in range(pattern_ref.shape[0]):
        q = pattern_ref[k : k + 1, :]
        inside = jnp.logical_and(q >= 32, q < 160)
        idx = jnp.where(q < 32, q, jnp.where(inside, q - 32, q - 128))
        idx = jnp.broadcast_to(idx, (width, LANES))
        inside = jnp.broadcast_to(inside, (width, LANES))
        picked_ref[k] = jnp.where(inside, gather_lanes(own, idx), gather_lanes(halo, idx))


def forward(curl_ref, picked_ref, face_ref, own_ref, previous_ref, sigma_ref, weight_ref, block_ref,
            sums_ref):
    kinds, rows, width, _ = curl_ref.shape
    tiles = block_ref.shape[0]
    sums_ref[...] = jnp.zeros_like(sums_ref)

    @pl.loop(0, rows // 8)
    def _(step):
        first = pl.multiple_of(step * 8, 8)
        total = None
        for k in range(kinds):
            for t in range(0, width, 8):
                term = curl_ref[k, pl.ds(first, 8), t : t + 8, :] * picked_ref[k, t : t + 8, :][None]
                total = term if total is None else total + term
        face_ref[pl.ds(first, 8), :] = jnp.sum(total, axis=1)
        own = own_ref[pl.ds(first, 8), :]
        for i in range(tiles):
            at = slice(i * LANES, (i + 1) * LANES)
            idx = jnp.broadcast_to(block_ref[i : i + 1, :], (8, LANES))
            sums_ref[i] += gather_lanes(own, idx) * weight_ref[pl.ds(first, 8), at]
        square = own * own
        sums_ref[tiles] += square
        sums_ref[tiles + 1] += sigma_ref[pl.ds(first, 8), :] * square
        if previous_ref is not None:
            sums_ref[tiles + 2] += own * previous_ref[pl.ds(first, 8), :]


def backward(curl_ref, bent_ref, back_ref, pat_ref, sigma_ref, own, centre_out, rim_out, msg_out):
    kinds, rows, width, _ = curl_ref.shape

    group = 3

    @pl.loop(0, kinds // group)
    def _(step):
        totals = [None] * group
        for a in range(rows):
            row = bent_ref[a : a + 1, :]
            for j in range(group):
                term = curl_ref[step * group + j, a] * row
                totals[j] = term if a == 0 else totals[j] + term
        for j, total in enumerate(totals):
            at = pl.multiple_of((step * group + j) * LANES, LANES)
            back_ref[:, pl.ds(at, LANES)] = split_rows(total)

    spread = add_halves(nt_dot(back_ref[...], pat_ref[...]))
    rim = spread[:, LANES:]
    centre = sigma_ref[...] * own + spread[:, :LANES]
    centre_out[...] = centre
    if rim_out is not None:
        rim_out[...] = rim
    lane = lane_iota(width)
    edges = jnp.logical_or(lane < 32, lane >= 96)
    msg_out[0:width, 0:LANES] = jnp.where(
        edges, centre, jnp.where(lane < 64, rim, pltpu.roll(rim, 64, 1))
    )


def total_of(x):
    return jnp.sum(jnp.sum(x, axis=0, keepdims=True), axis=1, keepdims=True)


def summed_row(sums_ref, energy, crossed, coil_hot_ref, row_out):
    tiles = coil_hot_ref.shape[1] // LANES
    link = jnp.concatenate(
        [jnp.sum(sums_ref[i], axis=0, keepdims=True) for i in range(tiles)], axis=1
    )
    high = link.astype(BF16).astype(F32)
    mid = (link - high).astype(BF16).astype(F32)
    low = link - high - mid
    sub = lax.broadcasted_iota(jnp.int32, (8, link.shape[1]), 0)
    terms = jnp.where(sub == 0, high, jnp.where(sub == 1, mid, jnp.where(sub == 2, low, 0.0)))
    line = jnp.sum(nt_dot(terms.astype(BF16), coil_hot_ref[...]), axis=0, keepdims=True)
    lane = lane_iota()
    line = line + jnp.where(lane == COILS, total_of(sums_ref[tiles]), 0.0)
    line = line + jnp.where(lane == COILS + 1, total_of(energy + sums_ref[tiles + 1]), 0.0)
    if crossed:
        line = line + jnp.where(lane == COILS + 2, total_of(sums_ref[tiles + 2]), 0.0)
    row_out[...] = jnp.broadcast_to(line, row_out.shape)


def face_side(refs, own_ref, halo, previous_ref, row_out, picked_ref, face_ref, sums_ref):
    sigma_ref, reluct_ref, curl_ref, pattern_ref, weight_ref, block_ref, coil_hot_ref = refs
    pick_edges(pattern_ref, own_ref[...], halo, picked_ref)
    forward(curl_ref, picked_ref, face_ref, own_ref, previous_ref, sigma_ref, weight_ref, block_ref,
            sums_ref)
    face = face_ref[...]
    bent = reluct_ref[...] * face
    face_ref[...] = bent
    energy = jnp.sum((bent * face).reshape(-1, 8, LANES), axis=0)
    summed_row(sums_ref, energy, previous_ref is not None, coil_hot_ref, row_out)


def pick(line, at):
    return jnp.sum(jnp.where(lane_iota() == at, line, 0.0), axis=1, keepdims=True)


def first_kernel(count, rhs_ref, even_ref, odd_ref, sigma_ref, reluct_ref, curl_ref, pattern_ref,
                 weight_ref, block_ref, coil_hot_ref, pat_ref, coil_ref,
                 row_ref, msg_ref, centre_ref, rim_ref, halo_ref,
                 picked_ref, face_ref, back_ref, sums_ref):
    left, right = sides(even_ref[...], odd_ref[...])
    halo = halo_of(left, right, count)
    halo_ref[...] = halo
    width = rhs_ref.shape[0]
    msg_ref[0:width, LANES:] = weight_ref[...]
    msg_ref[width:, :] = jnp.zeros_like(msg_ref[width:, :])
    msg_ref[width : width + 1, LANES:] = rows_of(block_ref[...]).astype(F32)
    msg_ref[width + 1 : width + 2, LANES:] = rows_of(coil_ref[...]).astype(F32)
    own = rhs_ref[...]
    refs = (sigma_ref, reluct_ref, curl_ref, pattern_ref, weight_ref, block_ref, coil_hot_ref)
    face_side(refs, rhs_ref, halo, None, row_ref, picked_ref, face_ref, sums_ref)
    backward(curl_ref, face_ref, back_ref, pat_ref, sigma_ref, own, centre_ref, rim_ref, msg_ref)


def scalars(rows_ref, inv_ref, scal_ref):
    total = jnp.sum(rows_ref[...], axis=0, keepdims=True)
    current = total * inv_ref[0:1, :]
    norm, energy = pick(total, COILS), pick(total, COILS + 1)
    energy = energy + jnp.sum(current * total, axis=1, keepdims=True)
    if scal_ref is None:
        beta = None
        curve = energy
    else:
        beta = norm / pick(scal_ref[0:1, :], 0)
        cross = pick(total, COILS + 2)
        curve = energy + 2.0 * beta * cross + beta * beta * pick(scal_ref[0:1, :], 1)
    lane = lane_iota()
    state = jnp.where(lane == 0, norm, jnp.where(lane == 1, curve, 0.0))
    return current, norm / curve, beta, state


def own_image(left, right, centre, weight, current, coils, blk):
    lane = lane_iota(*centre.shape)
    image = centre + jnp.where(lane < 32, pltpu.roll(left, 96, 1), 0.0)
    image = image + jnp.where(lane >= 96, pltpu.roll(right, 32, 1), 0.0)
    return image + add_halves(nt_dot(split_rows(weighted(weight, current, coils)), blk))


def step_kernel(count, first, last, *refs):
    names = ["rows", "even", "odd"] + ([] if first else ["evenc", "oddc"])
    names += ["centre", "rim", "res", "halo"] + ([] if first else ["dir", "img", "imgh", "sol", "scal"])
    names += ["inv", "blk", "sigma", "reluct", "curl", "pattern", "weight", "block", "coilhot", "pat",
              "coil"]
    names += ["row_o", "res_o", "dir_o", "img_o", "sol_o", "scal_o"]
    names += ["msg_o", "centre_o"] + ([] if last else ["rim_o", "halo_o", "imgh_o"])
    r = dict(zip(names, refs))
    scratch = refs[len(names):]
    width = r["res"].shape[0]
    current, alpha, beta, state = scalars(r["rows"], r["inv"], r.get("scal"))
    r["scal_o"][...] = jnp.broadcast_to(state, r["scal_o"].shape)

    left, right = sides(r["even"][0:width, 0:LANES], r["odd"][0:width, 0:LANES])
    image = own_image(left, right, r["centre"][...], r["weight"][...], current,
                      rows_of(r["coil"][...]), r["blk"][...])

    ce, co = (r["even"], r["odd"]) if first else (r["evenc"], r["oddc"])
    cl, cr = sides(ce[:, LANES:], co[:, LANES:])
    spot = jnp.concatenate(
        [cl[width : width + 1].astype(jnp.int32) - 96, cr[width : width + 1].astype(jnp.int32) + 32],
        axis=1,
    )
    amount = jnp.concatenate(
        [
            weighted(c[0:width], current, c[width + 1 : width + 2].astype(jnp.int32))
            for c in (cl, cr)
        ],
        axis=1,
    )
    beyond = add_halves(nt_dot(split_rows(amount), onehot(spot, LANES)))
    lane = lane_iota(width)
    moved = jnp.where(lane < 32, pltpu.roll(left, 32, 1), pltpu.roll(right, 32, 1))
    image_halo = (moved + r["rim"][...] + beyond) * halo_mask(count)

    old = r["res"][...]
    if first:
        direction = old
        r["sol_o"][...] = alpha * direction
    else:
        direction = old + beta * r["dir"][...]
        image = image + beta * r["img"][...]
        image_halo = image_halo + beta * r["imgh"][...]
        r["sol_o"][...] = r["sol"][...] + alpha * direction
    r["dir_o"][...] = direction
    r["img_o"][...] = image
    own = old - alpha * image
    halo = r["halo"][...] - alpha * image_halo
    r["res_o"][...] = own
    refs = tuple(r[k] for k in ("sigma", "reluct", "curl", "pattern", "weight", "block", "coilhot"))
    picked_ref, face_ref, back_ref, sums_ref = scratch
    face_side(refs, r["res_o"], halo, r["img_o"], r["row_o"], picked_ref, face_ref, sums_ref)
    if not last:
        r["imgh_o"][...] = image_halo
        r["halo_o"][...] = halo
        r["msg_o"][:, LANES:] = jnp.zeros_like(r["msg_o"][:, LANES:])
    backward(r["curl"], face_ref, back_ref, r["pat"], r["sigma"], own, r["centre_o"], r.get("rim_o"),
             r["msg_o"])


def last_kernel(rows_ref, even_ref, odd_ref, centre_ref, res_ref, dir_ref, img_ref, sol_ref, scal_ref,
                inv_ref, blk_ref, weight_ref, coil_ref, sol_out, res_out):
    current, alpha, beta, _ = scalars(rows_ref, inv_ref, scal_ref)
    left, right = sides(even_ref[:, 0:LANES], odd_ref[:, 0:LANES])
    image = own_image(left, right, centre_ref[...], weight_ref[...], current,
                      rows_of(coil_ref[...]), blk_ref[...])
    image = image + beta * img_ref[...]
    sol_out[...] = sol_ref[...] + alpha * (res_ref[...] + beta * dir_ref[...])
    res_out[...] = res_ref[...] - alpha * image


def call(kernel, args, outs, name, hbm=(), scratch=(), cost=None):
    args = [
        pltpu.with_memory_space_constraint(x, pltpu.HBM) if i in hbm else x
        for i, x in enumerate(args)
    ]
    if cost is not None:
        cost = pl.CostEstimate(flops=cost, transcendentals=0, bytes_accessed=1 << 20)
    return pl.pallas_call(
        kernel,
        name=name,
        in_specs=[
            pl.BlockSpec(memory_space=pltpu.HBM if i in hbm else VMEM) for i in range(len(args))
        ],
        out_specs=[pl.BlockSpec(memory_space=VMEM)] * len(outs),
        out_shape=[jax.ShapeDtypeStruct(s, d) for s, d in outs],
        scratch_shapes=list(scratch),
        cost_estimate=cost,
        compiler_params=pltpu.CompilerParams(vmem_limit_bytes=8 << 20),
    )(*args)


def body(count, right_side, sigma, reluctivity, curl_blocks, pattern, cond_weight, cond_block,
         cond_coil, coil_phase, coil_resistance, switch_state):
    width, blocks = right_side.shape
    kinds = pattern.shape[0]
    conductors = cond_weight.shape[1]
    block = cond_block.reshape(-1, LANES)
    coil = cond_coil.reshape(-1, LANES)
    phase = coil_phase.reshape(1, -1)
    ohm = coil_resistance.reshape(1, -1)
    tile = ((width, LANES), F32)

    inner = [(i, i ^ 1) for i in range(count)]
    outer = [(i, i + 1) for i in range(1, count - 1, 2)]
    outer = outer + [(b, a) for a, b in outer]

    def exchange(message):
        return lax.ppermute(message, "dom", outer), lax.ppermute(message, "dom", inner)

    def gather_rows(rows):
        return lax.all_to_all(rows, "dom", 0, 0, tiled=True)

    def like(x):
        return (x.shape, x.dtype)

    rhs, weight_v, block_v, coil_v = call(
        rhs_kernel,
        (right_side, cond_weight, block, coil, phase, ohm, switch_state),
        [tile, like(cond_weight), like(block), like(coil)],
        "rhs",
        hbm=range(7),
        scratch=[VMEM((width, LANES), F32), VMEM(phase.shape, phase.dtype), VMEM(ohm.shape, F32),
                 pltpu.SMEM(switch_state.shape, switch_state.dtype), VMEM((8, LANES), F32),
                 pltpu.SemaphoreType.DMA((7,))],
        cost=COST,
    )
    odd, even = exchange(rhs)
    pat, blk, coil_hot, inv, pattern_v, sigma_v, reluct_v = call(
        table_kernel,
        (pattern, ohm, sigma, reluctivity, block_v, coil_v),
        [((2 * LANES, kinds * LANES), BF16), ((LANES, conductors), BF16),
         ((LANES, conductors), BF16), ((8, LANES), F32), like(pattern), tile, tile],
        "tables",
        hbm=range(4),
        scratch=[VMEM(ohm.shape, F32), pltpu.SemaphoreType.DMA((4,))],
        cost=COST,
    )
    picked, faces = VMEM((kinds, width, LANES), F32), VMEM((width, LANES), F32)
    back = VMEM((2 * width, kinds * LANES), BF16)
    sums = VMEM((conductors // LANES + 3, 8, LANES), F32)
    shared = (sigma_v, reluct_v, curl_blocks, pattern_v, weight_v, block_v, coil_hot, pat, coil_v)
    line = ((count, LANES), F32)
    wide = ((width + 8, LANES + conductors), F32)
    row, message, centre, rim, halo = call(
        functools.partial(first_kernel, count),
        (rhs, even, odd) + shared,
        [line, wide, tile, tile, tile],
        "apply0",
        scratch=[picked, faces, back, sums],
    )
    odd_c, even_c = odd, even = exchange(message)
    rows = gather_rows(row)
    res, direction, image, image_halo, sol, scal = rhs, None, None, None, None, None
    for turn in range(1, ITERS):
        first, last = turn == 1, turn == ITERS - 1
        args = (rows, even, odd) + (() if first else (even_c, odd_c)) + (centre, rim, res, halo)
        args += () if first else (direction, image, image_halo, sol, scal)
        state = [line, tile, tile, tile, tile, ((8, LANES), F32)]
        state += [tile] * 2 if last else [((width, 3 * LANES), F32)] + [tile] * 4
        row, res, direction, image, sol, scal, message, centre, *rest = call(
            functools.partial(step_kernel, count, first, last),
            args + (inv, blk) + shared,
            state,
            "apply%d" % turn,
            scratch=[picked, faces, back, sums],
        )
        if not last:
            rim, halo, image_halo = rest
        odd, even = exchange(message)
        rows = gather_rows(row)
    sol, res = call(
        last_kernel,
        (rows, even, odd, centre, res, direction, image, sol, scal, inv, blk, weight_v, coil_v),
        [tile, tile],
        "finish",
    )
    return sol, res


def solution(mesh):
    return jax.shard_map(
        functools.partial(body, mesh.shape["dom"]),
        mesh=mesh,
        in_specs=(
            P(None, "dom"),
            P(None, "dom"),
            P(None, "dom"),
            P(None, None, None, "dom"),
            P(None, "dom"),
            P(None, "dom"),
            P("dom"),
            P("dom", None),
            P(),
            P(),
            P(),
        ),
        out_specs=(P(None, "dom"), P(None, "dom")),
        check_vma=False,
    )
```

```python
import functools

import jax
import jax.numpy as jnp
from jax import lax
from jax.experimental import pallas as pl
from jax.experimental.pallas import tpu as pltpu
from jax.sharding import PartitionSpec as P

ITERS = 3
LINK_SCALE = 16.0
LANES = 128
COILS = 84
COST = 1 << 34
F32 = jnp.float32
BF16 = jnp.bfloat16
VMEM = pltpu.VMEM


def gather_lanes(x, idx):
    dims = lax.GatherDimensionNumbers(
        offset_dims=(),
        collapsed_slice_dims=(1,),
        start_index_map=(1,),
        operand_batching_dims=(0,),
        start_indices_batching_dims=(0,),
    )
    return lax.gather(
        x,
        idx[..., None],
        dims,
        slice_sizes=(1, 1),
        mode=lax.GatherScatterMode.PROMISE_IN_BOUNDS,
    )


def lane_iota(rows=1, lanes=LANES):
    return lax.broadcasted_iota(jnp.int32, (rows, lanes), 1)


def nt_dot(a, b):
    return lax.dot_general(a, b, (((1,), (1,)), ((), ())), preferred_element_type=F32)


def split_rows(x):
    high = x.astype(BF16)
    low = (x - high.astype(F32)).astype(BF16)
    return jnp.concatenate([high, low], axis=0)


def add_halves(x):
    half = x.shape[0] // 2
    return x[:half] + x[half:]


def rows_of(ids):
    return jnp.concatenate([ids[i : i + 1] for i in range(ids.shape[0])], axis=1)


def onehot(ids, count):
    slots = lax.broadcasted_iota(jnp.int32, (count, ids.shape[1]), 0)
    return jnp.where(slots == ids, 1.0, 0.0).astype(BF16)


def weighted(weight, table, coils):
    parts = []
    wide = jnp.broadcast_to(table, (8, LANES))
    for i in range(coils.shape[1] // LANES):
        tile = coils[:, i * LANES : (i + 1) * LANES]
        got = gather_lanes(wide, jnp.broadcast_to(tile, (8, LANES)))
        cut = weight[:, i * LANES : (i + 1) * LANES]
        parts.append(cut * jnp.broadcast_to(got[0:1], cut.shape))
    return jnp.concatenate(parts, axis=1)


def pad_lanes(row, scratch):
    scratch[...] = jnp.zeros_like(scratch)
    scratch[0:1, 0 : row.shape[1]] = row
    return scratch[0:1, :]


def move(pairs, sems):
    copies = [pltpu.make_async_copy(src, dst, sems.at[i]) for i, (src, dst) in enumerate(pairs)]
    for copy in copies:
        copy.start()
    return copies


def rhs_kernel(
    side_hbm, weight_hbm, block_hbm, coil_hbm, phase_hbm, ohm_hbm, state_hbm,
    rhs_ref, weight_ref, block_ref, coil_ref,
    side_ref, phase_ref, ohm_ref, state_ref, pad_ref, sems,
):
    copies = move(
        [
            (coil_hbm, coil_ref),
            (phase_hbm, phase_ref),
            (ohm_hbm, ohm_ref),
            (state_hbm, state_ref),
            (weight_hbm, weight_ref),
            (block_hbm, block_ref),
            (side_hbm, side_ref),
        ],
        sems,
    )
    for copy in copies:
        copy.wait()
    s0, s1, s2 = (state_ref[i].astype(F32) for i in range(3))
    mean = (s0 + s1 + s2) / 3.0
    phase = phase_ref[...]
    volts = jnp.where(
        phase == 0,
        s0 - mean,
        jnp.where(phase == 1, s1 - mean, jnp.where(phase == 2, s2 - mean, 0.0)),
    )
    source = pad_lanes(LINK_SCALE * volts / ohm_ref[...], pad_ref)
    coils, blocks = rows_of(coil_ref[...]), rows_of(block_ref[...])
    spread = split_rows(weighted(weight_ref[...], source, coils))
    rhs_ref[...] = side_ref[...] + add_halves(nt_dot(spread, onehot(blocks, LANES)))


def table_kernel(
    pattern_hbm, ohm_hbm, sigma_hbm, reluct_hbm, block_ref, coil_ref,
    pat_ref, blk_ref, coil_hot_ref, inv_ref, pattern_ref, sigma_ref, reluct_ref,
    ohm_ref, sems,
):
    copies = move(
        [
            (pattern_hbm, pattern_ref),
            (ohm_hbm, ohm_ref),
            (sigma_hbm, sigma_ref),
            (reluct_hbm, reluct_ref),
        ],
        sems,
    )
    blk_ref[...] = onehot(rows_of(block_ref[...]), LANES)
    coil_hot_ref[...] = onehot(rows_of(coil_ref[...]), LANES)
    for copy in copies:
        copy.wait()
    for k in range(pattern_ref.shape[0]):
        q = pattern_ref[k : k + 1, :]
        slot = jnp.where(q < 32, q + 128, jnp.where(q < 160, q - 32, q))
        pat_ref[:, k * LANES : (k + 1) * LANES] = onehot(slot, 2 * LANES)
    inv_ref[...] = jnp.zeros_like(inv_ref)
    inv_ref[0:1, 0 : ohm_ref.shape[1]] = 1.0 / ohm_ref[...]


def sides(a, b):
    even = lax.rem(lax.axis_index("dom"), 2) == 0
    return jnp.where(even, b, a), jnp.where(even, a, b)


def halo_mask(count):
    me = lax.axis_index("dom")
    lane = lane_iota()
    left = jnp.where(me > 0, 1.0, 0.0)
    right = jnp.where(me < count - 1, 1.0, 0.0)
    return jnp.where(lane < 32, left, jnp.where(lane < 64, right, 0.0))


def halo_of(left, right, count):
    lane = lane_iota(*left.shape)
    moved = jnp.where(lane < 32, pltpu.roll(left, 32, 1), pltpu.roll(right, 32, 1))
    return moved * halo_mask(count)


def pick_edges(pattern_ref, own, halo, picked_ref):
    width = own.shape[0]
    for k in range(pattern_ref.shape[0]):
        q = pattern_ref[k : k + 1, :]
        inside = jnp.logical_and(q >= 32, q < 160)
        idx = jnp.where(q < 32, q, jnp.where(inside, q - 32, q - 128))
        idx = jnp.broadcast_to(idx, (width, LANES))
        inside = jnp.broadcast_to(inside, (width, LANES))
        picked_ref[k] = jnp.where(inside, gather_lanes(own, idx), gather_lanes(halo, idx))


def forward(curl_ref, picked_ref, face_ref, own_ref, previous_ref, sigma_ref, weight_ref, block_ref,
            sums_ref):
    kinds, rows, width, _ = curl_ref.shape
    tiles = block_ref.shape[0]
    sums_ref[...] = jnp.zeros_like(sums_ref)

    @pl.loop(0, rows // 8)
    def _(step):
        first = pl.multiple_of(step * 8, 8)
        total = None
        for k in range(kinds):
            for t in range(0, width, 8):
                term = curl_ref[k, pl.ds(first, 8), t : t + 8, :] * picked_ref[k, t : t + 8, :][None]
                total = term if total is None else total + term
        face_ref[pl.ds(first, 8), :] = jnp.sum(total, axis=1)
        own = own_ref[pl.ds(first, 8), :]
        for i in range(tiles):
            at = slice(i * LANES, (i + 1) * LANES)
            idx = jnp.broadcast_to(block_ref[i : i + 1, :], (8, LANES))
            sums_ref[i] += gather_lanes(own, idx) * weight_ref[pl.ds(first, 8), at]
        square = own * own
        sums_ref[tiles] += square
        sums_ref[tiles + 1] += sigma_ref[pl.ds(first, 8), :] * square
        if previous_ref is not None:
            sums_ref[tiles + 2] += own * previous_ref[pl.ds(first, 8), :]


def backward(curl_ref, bent_ref, back_ref, pat_ref, sigma_ref, own, centre_out, rim_out, msg_out):
    kinds, rows, width, _ = curl_ref.shape

    group = 3

    @pl.loop(0, kinds // group)
    def _(step):
        totals = [None] * group
        for a in range(rows):
            row = bent_ref[a : a + 1, :]
            for j in range(group):
                term = curl_ref[step * group + j, a] * row
                totals[j] = term if a == 0 else totals[j] + term
        for j, total in enumerate(totals):
            at = pl.multiple_of((step * group + j) * LANES, LANES)
            back_ref[:, pl.ds(at, LANES)] = split_rows(total)

    spread = add_halves(nt_dot(back_ref[...], pat_ref[...]))
    rim = spread[:, LANES:]
    centre = sigma_ref[...] * own + spread[:, :LANES]
    centre_out[...] = centre
    if rim_out is not None:
        rim_out[...] = rim
    lane = lane_iota(width)
    edges = jnp.logical_or(lane < 32, lane >= 96)
    msg_out[0:width, 0:LANES] = jnp.where(
        edges, centre, jnp.where(lane < 64, rim, pltpu.roll(rim, 64, 1))
    )


def total_of(x):
    return jnp.sum(jnp.sum(x, axis=0, keepdims=True), axis=1, keepdims=True)


def summed_row(sums_ref, energy, crossed, coil_hot_ref, row_out):
    tiles = coil_hot_ref.shape[1] // LANES
    link = jnp.concatenate(
        [jnp.sum(sums_ref[i], axis=0, keepdims=True) for i in range(tiles)], axis=1
    )
    high = link.astype(BF16).astype(F32)
    mid = (link - high).astype(BF16).astype(F32)
    low = link - high - mid
    sub = lax.broadcasted_iota(jnp.int32, (8, link.shape[1]), 0)
    terms = jnp.where(sub == 0, high, jnp.where(sub == 1, mid, jnp.where(sub == 2, low, 0.0)))
    line = jnp.sum(nt_dot(terms.astype(BF16), coil_hot_ref[...]), axis=0, keepdims=True)
    lane = lane_iota()
    line = line + jnp.where(lane == COILS, total_of(sums_ref[tiles]), 0.0)
    line = line + jnp.where(lane == COILS + 1, total_of(energy + sums_ref[tiles + 1]), 0.0)
    if crossed:
        line = line + jnp.where(lane == COILS + 2, total_of(sums_ref[tiles + 2]), 0.0)
    row_out[...] = jnp.broadcast_to(line, row_out.shape)


def face_side(refs, own_ref, halo, previous_ref, row_out, picked_ref, face_ref, sums_ref):
    sigma_ref, reluct_ref, curl_ref, pattern_ref, weight_ref, block_ref, coil_hot_ref = refs
    pick_edges(pattern_ref, own_ref[...], halo, picked_ref)
    forward(curl_ref, picked_ref, face_ref, own_ref, previous_ref, sigma_ref, weight_ref, block_ref,
            sums_ref)
    face = face_ref[...]
    bent = reluct_ref[...] * face
    face_ref[...] = bent
    energy = jnp.sum((bent * face).reshape(-1, 8, LANES), axis=0)
    summed_row(sums_ref, energy, previous_ref is not None, coil_hot_ref, row_out)


def pick(line, at):
    return jnp.sum(jnp.where(lane_iota() == at, line, 0.0), axis=1, keepdims=True)


def first_kernel(count, rhs_ref, odd_ref, even_ref, sigma_ref, reluct_ref, curl_ref, pattern_ref,
                 weight_ref, block_ref, coil_hot_ref, pat_ref, coil_ref,
                 row_ref, msg_ref, centre_ref, rim_ref, halo_ref,
                 picked_ref, face_ref, back_ref, sums_ref):
    left, right = sides(even_ref[...], odd_ref[...])
    halo = halo_of(left, right, count)
    halo_ref[...] = halo
    width = rhs_ref.shape[0]
    msg_ref[0:width, LANES:] = weight_ref[...]
    msg_ref[width:, :] = jnp.zeros_like(msg_ref[width:, :])
    msg_ref[width : width + 1, LANES:] = rows_of(block_ref[...]).astype(F32)
    msg_ref[width + 1 : width + 2, LANES:] = rows_of(coil_ref[...]).astype(F32)
    own = rhs_ref[...]
    refs = (sigma_ref, reluct_ref, curl_ref, pattern_ref, weight_ref, block_ref, coil_hot_ref)
    face_side(refs, rhs_ref, halo, None, row_ref, picked_ref, face_ref, sums_ref)
    backward(curl_ref, face_ref, back_ref, pat_ref, sigma_ref, own, centre_ref, rim_ref, msg_ref)


def scalars(rows_ref, inv_ref, scal_ref):
    total = jnp.sum(rows_ref[...], axis=0, keepdims=True)
    current = total * inv_ref[0:1, :]
    norm, energy = pick(total, COILS), pick(total, COILS + 1)
    energy = energy + jnp.sum(current * total, axis=1, keepdims=True)
    if scal_ref is None:
        beta = None
        curve = energy
    else:
        beta = norm / pick(scal_ref[0:1, :], 0)
        cross = pick(total, COILS + 2)
        curve = energy + 2.0 * beta * cross + beta * beta * pick(scal_ref[0:1, :], 1)
    lane = lane_iota()
    state = jnp.where(lane == 0, norm, jnp.where(lane == 1, curve, 0.0))
    return current, norm / curve, beta, state


def own_image(left, right, centre, weight, current, coils, blk):
    lane = lane_iota(*centre.shape)
    image = centre + jnp.where(lane < 32, pltpu.roll(left, 96, 1), 0.0)
    image = image + jnp.where(lane >= 96, pltpu.roll(right, 32, 1), 0.0)
    return image + add_halves(nt_dot(split_rows(weighted(weight, current, coils)), blk))


def step_kernel(count, first, last, *refs):
    names = ["rows", "odd", "even"] + ([] if first else ["oddc", "evenc"])
    names += ["centre", "rim", "res", "halo"] + ([] if first else ["dir", "img", "imgh", "sol", "scal"])
    names += ["inv", "blk", "sigma", "reluct", "curl", "pattern", "weight", "block", "coilhot", "pat",
              "coil"]
    names += ["row_o", "res_o", "dir_o", "img_o", "sol_o", "scal_o"]
    names += ["msg_o", "centre_o"] + ([] if last else ["rim_o", "halo_o", "imgh_o"])
    r = dict(zip(names, refs))
    scratch = refs[len(names):]
    width = r["res"].shape[0]
    current, alpha, beta, state = scalars(r["rows"], r["inv"], r.get("scal"))
    r["scal_o"][...] = jnp.broadcast_to(state, r["scal_o"].shape)

    left, right = sides(r["even"][0:width, 0:LANES], r["odd"][0:width, 0:LANES])
    image = own_image(left, right, r["centre"][...], r["weight"][...], current,
                      rows_of(r["coil"][...]), r["blk"][...])

    ce, co = (r["even"], r["odd"]) if first else (r["evenc"], r["oddc"])
    cl, cr = sides(ce[:, LANES:], co[:, LANES:])
    spot = jnp.concatenate(
        [cl[width : width + 1].astype(jnp.int32) - 96, cr[width : width + 1].astype(jnp.int32) + 32],
        axis=1,
    )
    amount = jnp.concatenate(
        [
            weighted(c[0:width], current, c[width + 1 : width + 2].astype(jnp.int32))
            for c in (cl, cr)
        ],
        axis=1,
    )
    beyond = add_halves(nt_dot(split_rows(amount), onehot(spot, LANES)))
    lane = lane_iota(width)
    moved = jnp.where(lane < 32, pltpu.roll(left, 32, 1), pltpu.roll(right, 32, 1))
    image_halo = (moved + r["rim"][...] + beyond) * halo_mask(count)

    old = r["res"][...]
    if first:
        direction = old
        r["sol_o"][...] = alpha * direction
    else:
        direction = old + beta * r["dir"][...]
        image = image + beta * r["img"][...]
        image_halo = image_halo + beta * r["imgh"][...]
        r["sol_o"][...] = r["sol"][...] + alpha * direction
    r["dir_o"][...] = direction
    r["img_o"][...] = image
    own = old - alpha * image
    halo = r["halo"][...] - alpha * image_halo
    r["res_o"][...] = own
    refs = tuple(r[k] for k in ("sigma", "reluct", "curl", "pattern", "weight", "block", "coilhot"))
    picked_ref, face_ref, back_ref, sums_ref = scratch
    face_side(refs, r["res_o"], halo, r["img_o"], r["row_o"], picked_ref, face_ref, sums_ref)
    if not last:
        r["imgh_o"][...] = image_halo
        r["halo_o"][...] = halo
        r["msg_o"][:, LANES:] = jnp.zeros_like(r["msg_o"][:, LANES:])
    backward(r["curl"], face_ref, back_ref, r["pat"], r["sigma"], own, r["centre_o"], r.get("rim_o"),
             r["msg_o"])


def last_kernel(rows_ref, odd_ref, even_ref, centre_ref, res_ref, dir_ref, img_ref, sol_ref, scal_ref,
                inv_ref, blk_ref, weight_ref, coil_ref, sol_out, res_out):
    current, alpha, beta, _ = scalars(rows_ref, inv_ref, scal_ref)
    left, right = sides(even_ref[:, 0:LANES], odd_ref[:, 0:LANES])
    image = own_image(left, right, centre_ref[...], weight_ref[...], current,
                      rows_of(coil_ref[...]), blk_ref[...])
    image = image + beta * img_ref[...]
    sol_out[...] = sol_ref[...] + alpha * (res_ref[...] + beta * dir_ref[...])
    res_out[...] = res_ref[...] - alpha * image


def call(kernel, args, outs, name, hbm=(), scratch=(), cost=None):
    args = [
        pltpu.with_memory_space_constraint(x, pltpu.HBM) if i in hbm else x
        for i, x in enumerate(args)
    ]
    if cost is not None:
        cost = pl.CostEstimate(flops=cost, transcendentals=0, bytes_accessed=1 << 20)
    return pl.pallas_call(
        kernel,
        name=name,
        in_specs=[
            pl.BlockSpec(memory_space=pltpu.HBM if i in hbm else VMEM) for i in range(len(args))
        ],
        out_specs=[pl.BlockSpec(memory_space=VMEM)] * len(outs),
        out_shape=[jax.ShapeDtypeStruct(s, d) for s, d in outs],
        scratch_shapes=list(scratch),
        cost_estimate=cost,
        compiler_params=pltpu.CompilerParams(vmem_limit_bytes=8 << 20),
    )(*args)


def body(count, right_side, sigma, reluctivity, curl_blocks, pattern, cond_weight, cond_block,
         cond_coil, coil_phase, coil_resistance, switch_state):
    width, blocks = right_side.shape
    kinds = pattern.shape[0]
    conductors = cond_weight.shape[1]
    block = cond_block.reshape(-1, LANES)
    coil = cond_coil.reshape(-1, LANES)
    phase = coil_phase.reshape(1, -1)
    ohm = coil_resistance.reshape(1, -1)
    tile = ((width, LANES), F32)

    inner = [(i, i ^ 1) for i in range(count)]
    outer = [(i, i + 1) for i in range(1, count - 1, 2)]
    outer = outer + [(b, a) for a, b in outer]

    def exchange(message):
        near = lax.ppermute(message, "dom", inner)
        return lax.ppermute(message, "dom", outer), near

    def gather_rows(rows):
        return lax.all_to_all(rows, "dom", 0, 0, tiled=True)

    def like(x):
        return (x.shape, x.dtype)

    rhs, weight_v, block_v, coil_v = call(
        rhs_kernel,
        (right_side, cond_weight, block, coil, phase, ohm, switch_state),
        [tile, like(cond_weight), like(block), like(coil)],
        "rhs",
        hbm=range(7),
        scratch=[VMEM((width, LANES), F32), VMEM(phase.shape, phase.dtype), VMEM(ohm.shape, F32),
                 pltpu.SMEM(switch_state.shape, switch_state.dtype), VMEM((8, LANES), F32),
                 pltpu.SemaphoreType.DMA((7,))],
        cost=COST,
    )
    odd, even = exchange(rhs)
    pat, blk, coil_hot, inv, pattern_v, sigma_v, reluct_v = call(
        table_kernel,
        (pattern, ohm, sigma, reluctivity, block_v, coil_v),
        [((2 * LANES, kinds * LANES), BF16), ((LANES, conductors), BF16),
         ((LANES, conductors), BF16), ((8, LANES), F32), like(pattern), tile, tile],
        "tables",
        hbm=range(4),
        scratch=[VMEM(ohm.shape, F32), pltpu.SemaphoreType.DMA((4,))],
        cost=COST,
    )
    picked, faces = VMEM((kinds, width, LANES), F32), VMEM((width, LANES), F32)
    back = VMEM((2 * width, kinds * LANES), BF16)
    sums = VMEM((conductors // LANES + 3, 8, LANES), F32)
    shared = (sigma_v, reluct_v, curl_blocks, pattern_v, weight_v, block_v, coil_hot, pat, coil_v)
    line = ((count, LANES), F32)
    wide = ((width + 8, LANES + conductors), F32)
    row, message, centre, rim, halo = call(
        functools.partial(first_kernel, count),
        (rhs, odd, even) + shared,
        [line, wide, tile, tile, tile],
        "apply0",
        scratch=[picked, faces, back, sums],
    )
    odd_c, even_c = odd, even = exchange(message)
    rows = gather_rows(row)
    res, direction, image, image_halo, sol, scal = rhs, None, None, None, None, None
    for turn in range(1, ITERS):
        first, last = turn == 1, turn == ITERS - 1
        args = (rows, odd, even) + (() if first else (odd_c, even_c)) + (centre, rim, res, halo)
        args += () if first else (direction, image, image_halo, sol, scal)
        state = [line, tile, tile, tile, tile, ((8, LANES), F32)]
        state += [tile] * 2 if last else [((width, 3 * LANES), F32)] + [tile] * 4
        row, res, direction, image, sol, scal, message, centre, *rest = call(
            functools.partial(step_kernel, count, first, last),
            args + (inv, blk) + shared,
            state,
            "apply%d" % turn,
            scratch=[picked, faces, back, sums],
        )
        if not last:
            rim, halo, image_halo = rest
        odd, even = exchange(message)
        rows = gather_rows(row)
    sol, res = call(
        last_kernel,
        (rows, odd, even, centre, res, direction, image, sol, scal, inv, blk, weight_v, coil_v),
        [tile, tile],
        "finish",
    )
    return sol, res


def solution(mesh):
    return jax.shard_map(
        functools.partial(body, mesh.shape["dom"]),
        mesh=mesh,
        in_specs=(
            P(None, "dom"),
            P(None, "dom"),
            P(None, "dom"),
            P(None, None, None, "dom"),
            P(None, "dom"),
            P(None, "dom"),
            P("dom"),
            P("dom", None),
            P(),
            P(),
            P(),
        ),
        out_specs=(P(None, "dom"), P(None, "dom")),
        check_vma=False,
    )
```

```python
import functools

import jax
import jax.numpy as jnp
from jax import lax
from jax.experimental import pallas as pl
from jax.experimental.pallas import tpu as pltpu
from jax.sharding import PartitionSpec as P

ITERS = 3
LINK_SCALE = 16.0
LANES = 128
COILS = 84
COST = 1 << 34
F32 = jnp.float32
BF16 = jnp.bfloat16
VMEM = pltpu.VMEM


def gather_lanes(x, idx):
    dims = lax.GatherDimensionNumbers(
        offset_dims=(),
        collapsed_slice_dims=(1,),
        start_index_map=(1,),
        operand_batching_dims=(0,),
        start_indices_batching_dims=(0,),
    )
    return lax.gather(
        x,
        idx[..., None],
        dims,
        slice_sizes=(1, 1),
        mode=lax.GatherScatterMode.PROMISE_IN_BOUNDS,
    )


def lane_iota(rows=1, lanes=LANES):
    return lax.broadcasted_iota(jnp.int32, (rows, lanes), 1)


def nt_dot(a, b):
    return lax.dot_general(a, b, (((1,), (1,)), ((), ())), preferred_element_type=F32)


def split_rows(x):
    high = x.astype(BF16)
    low = (x - high.astype(F32)).astype(BF16)
    return jnp.concatenate([high, low], axis=0)


def add_halves(x):
    half = x.shape[0] // 2
    return x[:half] + x[half:]


def rows_of(ids):
    return jnp.concatenate([ids[i : i + 1] for i in range(ids.shape[0])], axis=1)


def onehot(ids, count):
    slots = lax.broadcasted_iota(jnp.int32, (count, ids.shape[1]), 0)
    return jnp.where(slots == ids, 1.0, 0.0).astype(BF16)


def weighted(weight, table, coils):
    parts = []
    wide = jnp.broadcast_to(table, (8, LANES))
    for i in range(coils.shape[1] // LANES):
        tile = coils[:, i * LANES : (i + 1) * LANES]
        got = gather_lanes(wide, jnp.broadcast_to(tile, (8, LANES)))
        cut = weight[:, i * LANES : (i + 1) * LANES]
        parts.append(cut * jnp.broadcast_to(got[0:1], cut.shape))
    return jnp.concatenate(parts, axis=1)


def pad_lanes(row, scratch):
    scratch[...] = jnp.zeros_like(scratch)
    scratch[0:1, 0 : row.shape[1]] = row
    return scratch[0:1, :]


def move(pairs, sems):
    copies = [pltpu.make_async_copy(src, dst, sems.at[i]) for i, (src, dst) in enumerate(pairs)]
    for copy in copies:
        copy.start()
    return copies


def rhs_kernel(
    side_hbm, weight_hbm, block_hbm, coil_hbm, phase_hbm, ohm_hbm, state_hbm,
    rhs_ref, weight_ref, block_ref, coil_ref,
    side_ref, phase_ref, ohm_ref, state_ref, pad_ref, sems,
):
    copies = move(
        [
            (coil_hbm, coil_ref),
            (phase_hbm, phase_ref),
            (ohm_hbm, ohm_ref),
            (state_hbm, state_ref),
            (weight_hbm, weight_ref),
            (block_hbm, block_ref),
            (side_hbm, side_ref),
        ],
        sems,
    )
    for copy in copies:
        copy.wait()
    s0, s1, s2 = (state_ref[i].astype(F32) for i in range(3))
    mean = (s0 + s1 + s2) / 3.0
    phase = phase_ref[...]
    volts = jnp.where(
        phase == 0,
        s0 - mean,
        jnp.where(phase == 1, s1 - mean, jnp.where(phase == 2, s2 - mean, 0.0)),
    )
    source = pad_lanes(LINK_SCALE * volts / ohm_ref[...], pad_ref)
    coils, blocks = rows_of(coil_ref[...]), rows_of(block_ref[...])
    spread = split_rows(weighted(weight_ref[...], source, coils))
    rhs_ref[...] = side_ref[...] + add_halves(nt_dot(spread, onehot(blocks, LANES)))


def table_kernel(
    pattern_hbm, ohm_hbm, sigma_hbm, reluct_hbm, block_ref, coil_ref,
    pat_ref, blk_ref, coil_hot_ref, inv_ref, pattern_ref, sigma_ref, reluct_ref,
    ohm_ref, sems,
):
    copies = move(
        [
            (pattern_hbm, pattern_ref),
            (ohm_hbm, ohm_ref),
            (sigma_hbm, sigma_ref),
            (reluct_hbm, reluct_ref),
        ],
        sems,
    )
    blk_ref[...] = onehot(rows_of(block_ref[...]), LANES)
    coil_hot_ref[...] = onehot(rows_of(coil_ref[...]), LANES)
    for copy in copies:
        copy.wait()
    for k in range(pattern_ref.shape[0]):
        q = pattern_ref[k : k + 1, :]
        slot = jnp.where(q < 32, q + 128, jnp.where(q < 160, q - 32, q))
        pat_ref[:, k * LANES : (k + 1) * LANES] = onehot(slot, 2 * LANES)
    inv_ref[...] = jnp.zeros_like(inv_ref)
    inv_ref[0:1, 0 : ohm_ref.shape[1]] = 1.0 / ohm_ref[...]


def sides(a, b):
    even = lax.rem(lax.axis_index("dom"), 2) == 0
    return jnp.where(even, b, a), jnp.where(even, a, b)


def halo_mask(count):
    me = lax.axis_index("dom")
    lane = lane_iota()
    left = jnp.where(me > 0, 1.0, 0.0)
    right = jnp.where(me < count - 1, 1.0, 0.0)
    return jnp.where(lane < 32, left, jnp.where(lane < 64, right, 0.0))


def halo_of(left, right, count):
    lane = lane_iota(*left.shape)
    moved = jnp.where(lane < 32, pltpu.roll(left, 32, 1), pltpu.roll(right, 32, 1))
    return moved * halo_mask(count)


def pick_edges(pattern_ref, own, halo, picked_ref):
    width = own.shape[0]
    for k in range(pattern_ref.shape[0]):
        q = pattern_ref[k : k + 1, :]
        inside = jnp.logical_and(q >= 32, q < 160)
        idx = jnp.where(q < 32, q, jnp.where(inside, q - 32, q - 128))
        idx = jnp.broadcast_to(idx, (width, LANES))
        inside = jnp.broadcast_to(inside, (width, LANES))
        picked_ref[k] = jnp.where(inside, gather_lanes(own, idx), gather_lanes(halo, idx))


def forward(curl_ref, picked_ref, face_ref, own_ref, previous_ref, sigma_ref, weight_ref, block_ref,
            sums_ref):
    kinds, rows, width, _ = curl_ref.shape
    tiles = block_ref.shape[0]
    sums_ref[...] = jnp.zeros_like(sums_ref)

    @pl.loop(0, rows // 8)
    def _(step):
        first = pl.multiple_of(step * 8, 8)
        total = None
        for k in range(kinds):
            for t in range(0, width, 8):
                term = curl_ref[k, pl.ds(first, 8), t : t + 8, :] * picked_ref[k, t : t + 8, :][None]
                total = term if total is None else total + term
        face_ref[pl.ds(first, 8), :] = jnp.sum(total, axis=1)
        own = own_ref[pl.ds(first, 8), :]
        for i in range(tiles):
            at = slice(i * LANES, (i + 1) * LANES)
            idx = jnp.broadcast_to(block_ref[i : i + 1, :], (8, LANES))
            sums_ref[i] += gather_lanes(own, idx) * weight_ref[pl.ds(first, 8), at]
        square = own * own
        sums_ref[tiles] += square
        sums_ref[tiles + 1] += sigma_ref[pl.ds(first, 8), :] * square
        if previous_ref is not None:
            sums_ref[tiles + 2] += own * previous_ref[pl.ds(first, 8), :]


def backward(curl_ref, bent_ref, pat_ref, sigma_ref, own, centre_out, rim_out, msg_out):
    kinds, rows, width, _ = curl_ref.shape

    group = 3
    spread = None
    for base in range(0, kinds, group):
        totals = [None] * group
        for a in range(rows):
            row = bent_ref[a : a + 1, :]
            for j in range(group):
                term = curl_ref[base + j, a] * row
                totals[j] = term if a == 0 else totals[j] + term
        terms = jnp.concatenate([split_rows(total) for total in totals], axis=1)
        part = nt_dot(terms, pat_ref[:, base * LANES : (base + group) * LANES])
        spread = part if spread is None else spread + part
    spread = add_halves(spread)
    rim = spread[:, LANES:]
    centre = sigma_ref[...] * own + spread[:, :LANES]
    centre_out[...] = centre
    if rim_out is not None:
        rim_out[...] = rim
    lane = lane_iota(width)
    edges = jnp.logical_or(lane < 32, lane >= 96)
    msg_out[0:width, 0:LANES] = jnp.where(
        edges, centre, jnp.where(lane < 64, rim, pltpu.roll(rim, 64, 1))
    )


def total_of(x):
    return jnp.sum(jnp.sum(x, axis=0, keepdims=True), axis=1, keepdims=True)


def summed_row(sums_ref, energy, crossed, coil_hot_ref, row_out):
    tiles = coil_hot_ref.shape[1] // LANES
    link = jnp.concatenate(
        [jnp.sum(sums_ref[i], axis=0, keepdims=True) for i in range(tiles)], axis=1
    )
    high = link.astype(BF16).astype(F32)
    mid = (link - high).astype(BF16).astype(F32)
    low = link - high - mid
    sub = lax.broadcasted_iota(jnp.int32, (8, link.shape[1]), 0)
    terms = jnp.where(sub == 0, high, jnp.where(sub == 1, mid, jnp.where(sub == 2, low, 0.0)))
    line = jnp.sum(nt_dot(terms.astype(BF16), coil_hot_ref[...]), axis=0, keepdims=True)
    lane = lane_iota()
    line = line + jnp.where(lane == COILS, total_of(sums_ref[tiles]), 0.0)
    line = line + jnp.where(lane == COILS + 1, total_of(energy + sums_ref[tiles + 1]), 0.0)
    if crossed:
        line = line + jnp.where(lane == COILS + 2, total_of(sums_ref[tiles + 2]), 0.0)
    row_out[...] = jnp.broadcast_to(line, row_out.shape)


def face_side(refs, own_ref, halo, previous_ref, row_out, picked_ref, face_ref, sums_ref):
    sigma_ref, reluct_ref, curl_ref, pattern_ref, weight_ref, block_ref, coil_hot_ref = refs
    pick_edges(pattern_ref, own_ref[...], halo, picked_ref)
    forward(curl_ref, picked_ref, face_ref, own_ref, previous_ref, sigma_ref, weight_ref, block_ref,
            sums_ref)
    face = face_ref[...]
    bent = reluct_ref[...] * face
    face_ref[...] = bent
    energy = jnp.sum((bent * face).reshape(-1, 8, LANES), axis=0)
    summed_row(sums_ref, energy, previous_ref is not None, coil_hot_ref, row_out)


def pick(line, at):
    return jnp.sum(jnp.where(lane_iota() == at, line, 0.0), axis=1, keepdims=True)


def first_kernel(count, rhs_ref, odd_ref, even_ref, sigma_ref, reluct_ref, curl_ref, pattern_ref,
                 weight_ref, block_ref, coil_hot_ref, pat_ref, coil_ref,
                 row_ref, msg_ref, centre_ref, rim_ref, halo_ref,
                 picked_ref, face_ref, sums_ref):
    left, right = sides(even_ref[...], odd_ref[...])
    halo = halo_of(left, right, count)
    halo_ref[...] = halo
    width = rhs_ref.shape[0]
    msg_ref[0:width, LANES:] = weight_ref[...]
    msg_ref[width:, :] = jnp.zeros_like(msg_ref[width:, :])
    msg_ref[width : width + 1, LANES:] = rows_of(block_ref[...]).astype(F32)
    msg_ref[width + 1 : width + 2, LANES:] = rows_of(coil_ref[...]).astype(F32)
    own = rhs_ref[...]
    refs = (sigma_ref, reluct_ref, curl_ref, pattern_ref, weight_ref, block_ref, coil_hot_ref)
    face_side(refs, rhs_ref, halo, None, row_ref, picked_ref, face_ref, sums_ref)
    backward(curl_ref, face_ref, pat_ref, sigma_ref, own, centre_ref, rim_ref, msg_ref)


def scalars(rows_ref, inv_ref, scal_ref):
    total = jnp.sum(rows_ref[...], axis=0, keepdims=True)
    current = total * inv_ref[0:1, :]
    norm, energy = pick(total, COILS), pick(total, COILS + 1)
    energy = energy + jnp.sum(current * total, axis=1, keepdims=True)
    if scal_ref is None:
        beta = None
        curve = energy
    else:
        beta = norm / pick(scal_ref[0:1, :], 0)
        cross = pick(total, COILS + 2)
        curve = energy + 2.0 * beta * cross + beta * beta * pick(scal_ref[0:1, :], 1)
    lane = lane_iota()
    state = jnp.where(lane == 0, norm, jnp.where(lane == 1, curve, 0.0))
    return current, norm / curve, beta, state


def own_image(left, right, centre, weight, current, coils, blk):
    lane = lane_iota(*centre.shape)
    image = centre + jnp.where(lane < 32, pltpu.roll(left, 96, 1), 0.0)
    image = image + jnp.where(lane >= 96, pltpu.roll(right, 32, 1), 0.0)
    return image + add_halves(nt_dot(split_rows(weighted(weight, current, coils)), blk))


def step_kernel(count, first, last, *refs):
    names = ["rows", "odd", "even"] + ([] if first else ["oddc", "evenc"])
    names += ["centre", "rim", "res", "halo"] + ([] if first else ["dir", "img", "imgh", "sol", "scal"])
    names += ["inv", "blk", "sigma", "reluct", "curl", "pattern", "weight", "block", "coilhot", "pat",
              "coil"]
    names += ["row_o", "res_o", "dir_o", "img_o", "sol_o", "scal_o"]
    names += ["msg_o", "centre_o"] + ([] if last else ["rim_o", "halo_o", "imgh_o"])
    r = dict(zip(names, refs))
    scratch = refs[len(names):]
    width = r["res"].shape[0]
    current, alpha, beta, state = scalars(r["rows"], r["inv"], r.get("scal"))
    r["scal_o"][...] = jnp.broadcast_to(state, r["scal_o"].shape)

    left, right = sides(r["even"][0:width, 0:LANES], r["odd"][0:width, 0:LANES])
    image = own_image(left, right, r["centre"][...], r["weight"][...], current,
                      rows_of(r["coil"][...]), r["blk"][...])

    ce, co = (r["even"], r["odd"]) if first else (r["evenc"], r["oddc"])
    cl, cr = sides(ce[:, LANES:], co[:, LANES:])
    spot = jnp.concatenate(
        [cl[width : width + 1].astype(jnp.int32) - 96, cr[width : width + 1].astype(jnp.int32) + 32],
        axis=1,
    )
    amount = jnp.concatenate(
        [
            weighted(c[0:width], current, c[width + 1 : width + 2].astype(jnp.int32))
            for c in (cl, cr)
        ],
        axis=1,
    )
    beyond = add_halves(nt_dot(split_rows(amount), onehot(spot, LANES)))
    lane = lane_iota(width)
    moved = jnp.where(lane < 32, pltpu.roll(left, 32, 1), pltpu.roll(right, 32, 1))
    image_halo = (moved + r["rim"][...] + beyond) * halo_mask(count)

    old = r["res"][...]
    if first:
        direction = old
        r["sol_o"][...] = alpha * direction
    else:
        direction = old + beta * r["dir"][...]
        image = image + beta * r["img"][...]
        image_halo = image_halo + beta * r["imgh"][...]
        r["sol_o"][...] = r["sol"][...] + alpha * direction
    r["dir_o"][...] = direction
    r["img_o"][...] = image
    own = old - alpha * image
    halo = r["halo"][...] - alpha * image_halo
    r["res_o"][...] = own
    refs = tuple(r[k] for k in ("sigma", "reluct", "curl", "pattern", "weight", "block", "coilhot"))
    picked_ref, face_ref, sums_ref = scratch
    face_side(refs, r["res_o"], halo, r["img_o"], r["row_o"], picked_ref, face_ref, sums_ref)
    if not last:
        r["imgh_o"][...] = image_halo
        r["halo_o"][...] = halo
        r["msg_o"][:, LANES:] = jnp.zeros_like(r["msg_o"][:, LANES:])
    backward(r["curl"], face_ref, r["pat"], r["sigma"], own, r["centre_o"], r.get("rim_o"),
             r["msg_o"])


def last_kernel(rows_ref, odd_ref, even_ref, centre_ref, res_ref, dir_ref, img_ref, sol_ref, scal_ref,
                inv_ref, blk_ref, weight_ref, coil_ref, sol_out, res_out):
    current, alpha, beta, _ = scalars(rows_ref, inv_ref, scal_ref)
    left, right = sides(even_ref[:, 0:LANES], odd_ref[:, 0:LANES])
    image = own_image(left, right, centre_ref[...], weight_ref[...], current,
                      rows_of(coil_ref[...]), blk_ref[...])
    image = image + beta * img_ref[...]
    sol_out[...] = sol_ref[...] + alpha * (res_ref[...] + beta * dir_ref[...])
    res_out[...] = res_ref[...] - alpha * image


def call(kernel, args, outs, name, hbm=(), scratch=(), cost=None):
    args = [
        pltpu.with_memory_space_constraint(x, pltpu.HBM) if i in hbm else x
        for i, x in enumerate(args)
    ]
    if cost is not None:
        cost = pl.CostEstimate(flops=cost, transcendentals=0, bytes_accessed=1 << 20)
    return pl.pallas_call(
        kernel,
        name=name,
        in_specs=[
            pl.BlockSpec(memory_space=pltpu.HBM if i in hbm else VMEM) for i in range(len(args))
        ],
        out_specs=[pl.BlockSpec(memory_space=VMEM)] * len(outs),
        out_shape=[jax.ShapeDtypeStruct(s, d) for s, d in outs],
        scratch_shapes=list(scratch),
        cost_estimate=cost,
        compiler_params=pltpu.CompilerParams(vmem_limit_bytes=8 << 20),
    )(*args)


def body(count, right_side, sigma, reluctivity, curl_blocks, pattern, cond_weight, cond_block,
         cond_coil, coil_phase, coil_resistance, switch_state):
    width, blocks = right_side.shape
    kinds = pattern.shape[0]
    conductors = cond_weight.shape[1]
    block = cond_block.reshape(-1, LANES)
    coil = cond_coil.reshape(-1, LANES)
    phase = coil_phase.reshape(1, -1)
    ohm = coil_resistance.reshape(1, -1)
    tile = ((width, LANES), F32)

    inner = [(i, i ^ 1) for i in range(count)]
    outer = [(i, i + 1) for i in range(1, count - 1, 2)]
    outer = outer + [(b, a) for a, b in outer]

    def exchange(message):
        near = lax.ppermute(message, "dom", inner)
        return lax.ppermute(message, "dom", outer), near

    def gather_rows(rows):
        return lax.all_to_all(rows, "dom", 0, 0, tiled=True)

    def like(x):
        return (x.shape, x.dtype)

    rhs, weight_v, block_v, coil_v = call(
        rhs_kernel,
        (right_side, cond_weight, block, coil, phase, ohm, switch_state),
        [tile, like(cond_weight), like(block), like(coil)],
        "rhs",
        hbm=range(7),
        scratch=[VMEM((width, LANES), F32), VMEM(phase.shape, phase.dtype), VMEM(ohm.shape, F32),
                 pltpu.SMEM(switch_state.shape, switch_state.dtype), VMEM((8, LANES), F32),
                 pltpu.SemaphoreType.DMA((7,))],
        cost=COST,
    )
    odd, even = exchange(rhs)
    pat, blk, coil_hot, inv, pattern_v, sigma_v, reluct_v = call(
        table_kernel,
        (pattern, ohm, sigma, reluctivity, block_v, coil_v),
        [((2 * LANES, kinds * LANES), BF16), ((LANES, conductors), BF16),
         ((LANES, conductors), BF16), ((8, LANES), F32), like(pattern), tile, tile],
        "tables",
        hbm=range(4),
        scratch=[VMEM(ohm.shape, F32), pltpu.SemaphoreType.DMA((4,))],
        cost=COST,
    )
    picked, faces = VMEM((kinds, width, LANES), F32), VMEM((width, LANES), F32)
    sums = VMEM((conductors // LANES + 3, 8, LANES), F32)
    shared = (sigma_v, reluct_v, curl_blocks, pattern_v, weight_v, block_v, coil_hot, pat, coil_v)
    line = ((count, LANES), F32)
    wide = ((width + 8, LANES + conductors), F32)
    row, message, centre, rim, halo = call(
        functools.partial(first_kernel, count),
        (rhs, odd, even) + shared,
        [line, wide, tile, tile, tile],
        "apply0",
        scratch=[picked, faces, sums],
    )
    odd_c, even_c = odd, even = exchange(message)
    rows = gather_rows(row)
    res, direction, image, image_halo, sol, scal = rhs, None, None, None, None, None
    for turn in range(1, ITERS):
        first, last = turn == 1, turn == ITERS - 1
        args = (rows, odd, even) + (() if first else (odd_c, even_c)) + (centre, rim, res, halo)
        args += () if first else (direction, image, image_halo, sol, scal)
        state = [line, tile, tile, tile, tile, ((8, LANES), F32)]
        state += [tile] * 2 if last else [((width, 3 * LANES), F32)] + [tile] * 4
        row, res, direction, image, sol, scal, message, centre, *rest = call(
            functools.partial(step_kernel, count, first, last),
            args + (inv, blk) + shared,
            state,
            "apply%d" % turn,
            scratch=[picked, faces, sums],
        )
        if not last:
            rim, halo, image_halo = rest
        odd, even = exchange(message)
        rows = gather_rows(row)
    sol, res = call(
        last_kernel,
        (rows, odd, even, centre, res, direction, image, sol, scal, inv, blk, weight_v, coil_v),
        [tile, tile],
        "finish",
    )
    return sol, res


def solution(mesh):
    return jax.shard_map(
        functools.partial(body, mesh.shape["dom"]),
        mesh=mesh,
        in_specs=(
            P(None, "dom"),
            P(None, "dom"),
            P(None, "dom"),
            P(None, None, None, "dom"),
            P(None, "dom"),
            P(None, "dom"),
            P("dom"),
            P("dom", None),
            P(),
            P(),
            P(),
        ),
        out_specs=(P(None, "dom"), P(None, "dom")),
        check_vma=False,
    )
```

```python
import functools

import jax
import jax.numpy as jnp
from jax import lax
from jax.experimental import pallas as pl
from jax.experimental.pallas import tpu as pltpu
from jax.sharding import PartitionSpec as P

ITERS = 3
LINK_SCALE = 16.0
LANES = 128
COILS = 84
COST = 1 << 34
F32 = jnp.float32
BF16 = jnp.bfloat16
VMEM = pltpu.VMEM


def gather_lanes(x, idx):
    dims = lax.GatherDimensionNumbers(
        offset_dims=(),
        collapsed_slice_dims=(1,),
        start_index_map=(1,),
        operand_batching_dims=(0,),
        start_indices_batching_dims=(0,),
    )
    return lax.gather(
        x,
        idx[..., None],
        dims,
        slice_sizes=(1, 1),
        mode=lax.GatherScatterMode.PROMISE_IN_BOUNDS,
    )


def lane_iota(rows=1, lanes=LANES):
    return lax.broadcasted_iota(jnp.int32, (rows, lanes), 1)


def nt_dot(a, b):
    return lax.dot_general(a, b, (((1,), (1,)), ((), ())), preferred_element_type=F32)


def split_rows(x):
    high = x.astype(BF16)
    low = (x - high.astype(F32)).astype(BF16)
    return jnp.concatenate([high, low], axis=0)


def add_halves(x):
    half = x.shape[0] // 2
    return x[:half] + x[half:]


def rows_of(ids):
    return jnp.concatenate([ids[i : i + 1] for i in range(ids.shape[0])], axis=1)


def onehot(ids, count):
    slots = lax.broadcasted_iota(jnp.int32, (count, ids.shape[1]), 0)
    return jnp.where(slots == ids, 1.0, 0.0).astype(BF16)


def weighted(weight, table, coils):
    parts = []
    wide = jnp.broadcast_to(table, (8, LANES))
    for i in range(coils.shape[1] // LANES):
        tile = coils[:, i * LANES : (i + 1) * LANES]
        got = gather_lanes(wide, jnp.broadcast_to(tile, (8, LANES)))
        cut = weight[:, i * LANES : (i + 1) * LANES]
        parts.append(cut * jnp.broadcast_to(got[0:1], cut.shape))
    return jnp.concatenate(parts, axis=1)


def pad_lanes(row, scratch):
    scratch[...] = jnp.zeros_like(scratch)
    scratch[0:1, 0 : row.shape[1]] = row
    return scratch[0:1, :]


def move(pairs, sems):
    copies = [pltpu.make_async_copy(src, dst, sems.at[i]) for i, (src, dst) in enumerate(pairs)]
    for copy in copies:
        copy.start()
    return copies


def rhs_kernel(
    side_hbm, weight_hbm, block_hbm, coil_hbm, phase_hbm, ohm_hbm, state_hbm,
    rhs_ref, weight_ref, block_ref, coil_ref,
    side_ref, phase_ref, ohm_ref, state_ref, pad_ref, sems,
):
    copies = move(
        [
            (weight_hbm, weight_ref),
            (coil_hbm, coil_ref),
            (phase_hbm, phase_ref),
            (ohm_hbm, ohm_ref),
            (state_hbm, state_ref),
            (block_hbm, block_ref),
            (side_hbm, side_ref),
        ],
        sems,
    )
    for copy in copies[1:6]:
        copy.wait()
    s0, s1, s2 = (state_ref[i].astype(F32) for i in range(3))
    mean = (s0 + s1 + s2) / 3.0
    phase = phase_ref[...]
    volts = jnp.where(
        phase == 0,
        s0 - mean,
        jnp.where(phase == 1, s1 - mean, jnp.where(phase == 2, s2 - mean, 0.0)),
    )
    source = pad_lanes(LINK_SCALE * volts / ohm_ref[...], pad_ref)
    wide = jnp.broadcast_to(source, (8, LANES))
    coils = coil_ref[...]
    rows = [
        gather_lanes(wide, jnp.broadcast_to(coils[i : i + 1], (8, LANES)))[0:1]
        for i in range(coils.shape[0])
    ]
    amount = jnp.concatenate(rows, axis=1)
    hot = onehot(rows_of(block_ref[...]), LANES)
    copies[0].wait()
    copies[6].wait()
    spread = split_rows(weight_ref[...] * amount)
    rhs_ref[...] = side_ref[...] + add_halves(nt_dot(spread, hot))


def table_kernel(
    pattern_hbm, ohm_hbm, sigma_hbm, reluct_hbm, block_ref, coil_ref,
    pat_ref, blk_ref, coil_hot_ref, inv_ref, pattern_ref, sigma_ref, reluct_ref,
    ohm_ref, sems,
):
    copies = move(
        [
            (pattern_hbm, pattern_ref),
            (ohm_hbm, ohm_ref),
            (sigma_hbm, sigma_ref),
            (reluct_hbm, reluct_ref),
        ],
        sems,
    )
    blk_ref[...] = onehot(rows_of(block_ref[...]), LANES)
    coil_hot_ref[...] = onehot(rows_of(coil_ref[...]), LANES)
    for copy in copies:
        copy.wait()
    for k in range(pattern_ref.shape[0]):
        q = pattern_ref[k : k + 1, :]
        slot = jnp.where(q < 32, q + 128, jnp.where(q < 160, q - 32, q))
        pat_ref[:, k * LANES : (k + 1) * LANES] = onehot(slot, 2 * LANES)
    inv_ref[...] = jnp.zeros_like(inv_ref)
    inv_ref[0:1, 0 : ohm_ref.shape[1]] = 1.0 / ohm_ref[...]


def sides(a, b):
    even = lax.rem(lax.axis_index("dom"), 2) == 0
    return jnp.where(even, b, a), jnp.where(even, a, b)


def halo_mask(count):
    me = lax.axis_index("dom")
    lane = lane_iota()
    left = jnp.where(me > 0, 1.0, 0.0)
    right = jnp.where(me < count - 1, 1.0, 0.0)
    return jnp.where(lane < 32, left, jnp.where(lane < 64, right, 0.0))


def halo_of(left, right, count):
    lane = lane_iota(*left.shape)
    moved = jnp.where(lane < 32, pltpu.roll(left, 32, 1), pltpu.roll(right, 32, 1))
    return moved * halo_mask(count)


def pick_edges(pattern_ref, own, halo, picked_ref):
    width = own.shape[0]
    for k in range(pattern_ref.shape[0]):
        q = pattern_ref[k : k + 1, :]
        inside = jnp.logical_and(q >= 32, q < 160)
        idx = jnp.where(q < 32, q, jnp.where(inside, q - 32, q - 128))
        idx = jnp.broadcast_to(idx, (width, LANES))
        inside = jnp.broadcast_to(inside, (width, LANES))
        picked_ref[k] = jnp.where(inside, gather_lanes(own, idx), gather_lanes(halo, idx))


def forward(curl_ref, picked_ref, face_ref, own_ref, previous_ref, sigma_ref, weight_ref, block_ref,
            sums_ref):
    kinds, rows, width, _ = curl_ref.shape
    tiles = block_ref.shape[0]
    sums_ref[...] = jnp.zeros_like(sums_ref)

    @pl.loop(0, rows // 8)
    def _(step):
        first = pl.multiple_of(step * 8, 8)
        total = None
        for k in range(kinds):
            for t in range(0, width, 8):
                term = curl_ref[k, pl.ds(first, 8), t : t + 8, :] * picked_ref[k, t : t + 8, :][None]
                total = term if total is None else total + term
        face_ref[pl.ds(first, 8), :] = jnp.sum(total, axis=1)
        own = own_ref[pl.ds(first, 8), :]
        for i in range(tiles):
            at = slice(i * LANES, (i + 1) * LANES)
            idx = jnp.broadcast_to(block_ref[i : i + 1, :], (8, LANES))
            sums_ref[i] += gather_lanes(own, idx) * weight_ref[pl.ds(first, 8), at]
        square = own * own
        sums_ref[tiles] += square
        sums_ref[tiles + 1] += sigma_ref[pl.ds(first, 8), :] * square
        if previous_ref is not None:
            sums_ref[tiles + 2] += own * previous_ref[pl.ds(first, 8), :]


def backward(curl_ref, bent_ref, pat_ref, sigma_ref, own, centre_out, rim_out, msg_out):
    kinds, rows, width, _ = curl_ref.shape

    group = 3
    spread = None
    for base in range(0, kinds, group):
        totals = [None] * group
        for a in range(rows):
            row = bent_ref[a : a + 1, :]
            for j in range(group):
                term = curl_ref[base + j, a] * row
                totals[j] = term if a == 0 else totals[j] + term
        terms = jnp.concatenate([split_rows(total) for total in totals], axis=1)
        part = nt_dot(terms, pat_ref[:, base * LANES : (base + group) * LANES])
        spread = part if spread is None else spread + part
    spread = add_halves(spread)
    rim = spread[:, LANES:]
    centre = sigma_ref[...] * own + spread[:, :LANES]
    centre_out[...] = centre
    if rim_out is not None:
        rim_out[...] = rim
    lane = lane_iota(width)
    edges = jnp.logical_or(lane < 32, lane >= 96)
    msg_out[0:width, 0:LANES] = jnp.where(
        edges, centre, jnp.where(lane < 64, rim, pltpu.roll(rim, 64, 1))
    )


def total_of(x):
    return jnp.sum(jnp.sum(x, axis=0, keepdims=True), axis=1, keepdims=True)


def summed_row(sums_ref, energy, crossed, coil_hot_ref, row_out):
    tiles = coil_hot_ref.shape[1] // LANES
    link = jnp.concatenate(
        [jnp.sum(sums_ref[i], axis=0, keepdims=True) for i in range(tiles)], axis=1
    )
    high = link.astype(BF16).astype(F32)
    mid = (link - high).astype(BF16).astype(F32)
    low = link - high - mid
    sub = lax.broadcasted_iota(jnp.int32, (8, link.shape[1]), 0)
    terms = jnp.where(sub == 0, high, jnp.where(sub == 1, mid, jnp.where(sub == 2, low, 0.0)))
    line = jnp.sum(nt_dot(terms.astype(BF16), coil_hot_ref[...]), axis=0, keepdims=True)
    lane = lane_iota()
    line = line + jnp.where(lane == COILS, total_of(sums_ref[tiles]), 0.0)
    line = line + jnp.where(lane == COILS + 1, total_of(energy + sums_ref[tiles + 1]), 0.0)
    if crossed:
        line = line + jnp.where(lane == COILS + 2, total_of(sums_ref[tiles + 2]), 0.0)
    row_out[...] = jnp.broadcast_to(line, row_out.shape)


def face_side(refs, own_ref, halo, previous_ref, row_out, picked_ref, face_ref, sums_ref):
    sigma_ref, reluct_ref, curl_ref, pattern_ref, weight_ref, block_ref, coil_hot_ref = refs
    pick_edges(pattern_ref, own_ref[...], halo, picked_ref)
    forward(curl_ref, picked_ref, face_ref, own_ref, previous_ref, sigma_ref, weight_ref, block_ref,
            sums_ref)
    face = face_ref[...]
    bent = reluct_ref[...] * face
    face_ref[...] = bent
    energy = jnp.sum((bent * face).reshape(-1, 8, LANES), axis=0)
    summed_row(sums_ref, energy, previous_ref is not None, coil_hot_ref, row_out)


def pick(line, at):
    return jnp.sum(jnp.where(lane_iota() == at, line, 0.0), axis=1, keepdims=True)


def first_kernel(count, rhs_ref, odd_ref, even_ref, sigma_ref, reluct_ref, curl_ref, pattern_ref,
                 weight_ref, block_ref, coil_hot_ref, pat_ref, coil_ref,
                 row_ref, msg_ref, centre_ref, rim_ref, halo_ref,
                 picked_ref, face_ref, sums_ref):
    left, right = sides(even_ref[...], odd_ref[...])
    halo = halo_of(left, right, count)
    halo_ref[...] = halo
    width = rhs_ref.shape[0]
    msg_ref[0:width, LANES:] = weight_ref[...]
    msg_ref[width:, :] = jnp.zeros_like(msg_ref[width:, :])
    msg_ref[width : width + 1, LANES:] = rows_of(block_ref[...]).astype(F32)
    msg_ref[width + 1 : width + 2, LANES:] = rows_of(coil_ref[...]).astype(F32)
    own = rhs_ref[...]
    refs = (sigma_ref, reluct_ref, curl_ref, pattern_ref, weight_ref, block_ref, coil_hot_ref)
    face_side(refs, rhs_ref, halo, None, row_ref, picked_ref, face_ref, sums_ref)
    backward(curl_ref, face_ref, pat_ref, sigma_ref, own, centre_ref, rim_ref, msg_ref)


def scalars(rows_ref, inv_ref, scal_ref):
    total = jnp.sum(rows_ref[...], axis=0, keepdims=True)
    current = total * inv_ref[0:1, :]
    norm, energy = pick(total, COILS), pick(total, COILS + 1)
    energy = energy + jnp.sum(current * total, axis=1, keepdims=True)
    if scal_ref is None:
        beta = None
        curve = energy
    else:
        beta = norm / pick(scal_ref[0:1, :], 0)
        cross = pick(total, COILS + 2)
        curve = energy + 2.0 * beta * cross + beta * beta * pick(scal_ref[0:1, :], 1)
    lane = lane_iota()
    state = jnp.where(lane == 0, norm, jnp.where(lane == 1, curve, 0.0))
    return current, norm / curve, beta, state


def own_image(left, right, centre, weight, current, coils, blk):
    lane = lane_iota(*centre.shape)
    image = centre + jnp.where(lane < 32, pltpu.roll(left, 96, 1), 0.0)
    image = image + jnp.where(lane >= 96, pltpu.roll(right, 32, 1), 0.0)
    return image + add_halves(nt_dot(split_rows(weighted(weight, current, coils)), blk))


def step_kernel(count, first, last, *refs):
    names = ["rows", "odd", "even"] + ([] if first else ["oddc", "evenc"])
    names += ["centre", "rim", "res", "halo"] + ([] if first else ["dir", "img", "imgh", "sol", "scal"])
    names += ["inv", "blk", "sigma", "reluct", "curl", "pattern", "weight", "block", "coilhot", "pat",
              "coil"]
    names += ["row_o", "res_o", "dir_o", "img_o", "sol_o", "scal_o"]
    names += ["msg_o", "centre_o"] + ([] if last else ["rim_o", "halo_o", "imgh_o"])
    r = dict(zip(names, refs))
    scratch = refs[len(names):]
    width = r["res"].shape[0]
    current, alpha, beta, state = scalars(r["rows"], r["inv"], r.get("scal"))
    r["scal_o"][...] = jnp.broadcast_to(state, r["scal_o"].shape)

    left, right = sides(r["even"][0:width, 0:LANES], r["odd"][0:width, 0:LANES])
    image = own_image(left, right, r["centre"][...], r["weight"][...], current,
                      rows_of(r["coil"][...]), r["blk"][...])

    ce, co = (r["even"], r["odd"]) if first else (r["evenc"], r["oddc"])
    cl, cr = sides(ce[:, LANES:], co[:, LANES:])
    spot = jnp.concatenate(
        [cl[width : width + 1].astype(jnp.int32) - 96, cr[width : width + 1].astype(jnp.int32) + 32],
        axis=1,
    )
    amount = jnp.concatenate(
        [
            weighted(c[0:width], current, c[width + 1 : width + 2].astype(jnp.int32))
            for c in (cl, cr)
        ],
        axis=1,
    )
    beyond = add_halves(nt_dot(split_rows(amount), onehot(spot, LANES)))
    lane = lane_iota(width)
    moved = jnp.where(lane < 32, pltpu.roll(left, 32, 1), pltpu.roll(right, 32, 1))
    image_halo = (moved + r["rim"][...] + beyond) * halo_mask(count)

    old = r["res"][...]
    if first:
        direction = old
        r["sol_o"][...] = alpha * direction
    else:
        direction = old + beta * r["dir"][...]
        image = image + beta * r["img"][...]
        image_halo = image_halo + beta * r["imgh"][...]
        r["sol_o"][...] = r["sol"][...] + alpha * direction
    r["dir_o"][...] = direction
    r["img_o"][...] = image
    own = old - alpha * image
    halo = r["halo"][...] - alpha * image_halo
    r["res_o"][...] = own
    refs = tuple(r[k] for k in ("sigma", "reluct", "curl", "pattern", "weight", "block", "coilhot"))
    picked_ref, face_ref, sums_ref = scratch
    face_side(refs, r["res_o"], halo, r["img_o"], r["row_o"], picked_ref, face_ref, sums_ref)
    if not last:
        r["imgh_o"][...] = image_halo
        r["halo_o"][...] = halo
        r["msg_o"][:, LANES:] = jnp.zeros_like(r["msg_o"][:, LANES:])
    backward(r["curl"], face_ref, r["pat"], r["sigma"], own, r["centre_o"], r.get("rim_o"),
             r["msg_o"])


def last_kernel(rows_ref, odd_ref, even_ref, centre_ref, res_ref, dir_ref, img_ref, sol_ref, scal_ref,
                inv_ref, blk_ref, weight_ref, coil_ref, sol_out, res_out):
    current, alpha, beta, _ = scalars(rows_ref, inv_ref, scal_ref)
    left, right = sides(even_ref[:, 0:LANES], odd_ref[:, 0:LANES])
    image = own_image(left, right, centre_ref[...], weight_ref[...], current,
                      rows_of(coil_ref[...]), blk_ref[...])
    image = image + beta * img_ref[...]
    sol_out[...] = sol_ref[...] + alpha * (res_ref[...] + beta * dir_ref[...])
    res_out[...] = res_ref[...] - alpha * image


def call(kernel, args, outs, name, hbm=(), scratch=(), cost=None):
    args = [
        pltpu.with_memory_space_constraint(x, pltpu.HBM) if i in hbm else x
        for i, x in enumerate(args)
    ]
    if cost is not None:
        cost = pl.CostEstimate(flops=cost, transcendentals=0, bytes_accessed=1 << 20)
    return pl.pallas_call(
        kernel,
        name=name,
        in_specs=[
            pl.BlockSpec(memory_space=pltpu.HBM if i in hbm else VMEM) for i in range(len(args))
        ],
        out_specs=[pl.BlockSpec(memory_space=VMEM)] * len(outs),
        out_shape=[jax.ShapeDtypeStruct(s, d) for s, d in outs],
        scratch_shapes=list(scratch),
        cost_estimate=cost,
        compiler_params=pltpu.CompilerParams(vmem_limit_bytes=8 << 20),
    )(*args)


def body(count, right_side, sigma, reluctivity, curl_blocks, pattern, cond_weight, cond_block,
         cond_coil, coil_phase, coil_resistance, switch_state):
    width, blocks = right_side.shape
    kinds = pattern.shape[0]
    conductors = cond_weight.shape[1]
    block = cond_block.reshape(-1, LANES)
    coil = cond_coil.reshape(-1, LANES)
    phase = coil_phase.reshape(1, -1)
    ohm = coil_resistance.reshape(1, -1)
    tile = ((width, LANES), F32)

    inner = [(i, i ^ 1) for i in range(count)]
    outer = [(i, i + 1) for i in range(1, count - 1, 2)]
    outer = outer + [(b, a) for a, b in outer]

    def exchange(message):
        near = lax.ppermute(message, "dom", inner)
        return lax.ppermute(message, "dom", outer), near

    def gather_rows(rows):
        return lax.all_to_all(rows, "dom", 0, 0, tiled=True)

    def like(x):
        return (x.shape, x.dtype)

    rhs, weight_v, block_v, coil_v = call(
        rhs_kernel,
        (right_side, cond_weight, block, coil, phase, ohm, switch_state),
        [tile, like(cond_weight), like(block), like(coil)],
        "rhs",
        hbm=range(7),
        scratch=[VMEM((width, LANES), F32), VMEM(phase.shape, phase.dtype), VMEM(ohm.shape, F32),
                 pltpu.SMEM(switch_state.shape, switch_state.dtype), VMEM((8, LANES), F32),
                 pltpu.SemaphoreType.DMA((7,))],
        cost=COST,
    )
    odd, even = exchange(rhs)
    pat, blk, coil_hot, inv, pattern_v, sigma_v, reluct_v = call(
        table_kernel,
        (pattern, ohm, sigma, reluctivity, block_v, coil_v),
        [((2 * LANES, kinds * LANES), BF16), ((LANES, conductors), BF16),
         ((LANES, conductors), BF16), ((8, LANES), F32), like(pattern), tile, tile],
        "tables",
        hbm=range(4),
        scratch=[VMEM(ohm.shape, F32), pltpu.SemaphoreType.DMA((4,))],
        cost=COST,
    )
    picked, faces = VMEM((kinds, width, LANES), F32), VMEM((width, LANES), F32)
    sums = VMEM((conductors // LANES + 3, 8, LANES), F32)
    shared = (sigma_v, reluct_v, curl_blocks, pattern_v, weight_v, block_v, coil_hot, pat, coil_v)
    line = ((count, LANES), F32)
    wide = ((width + 8, LANES + conductors), F32)
    row, message, centre, rim, halo = call(
        functools.partial(first_kernel, count),
        (rhs, odd, even) + shared,
        [line, wide, tile, tile, tile],
        "apply0",
        scratch=[picked, faces, sums],
    )
    odd_c, even_c = odd, even = exchange(message)
    rows = gather_rows(row)
    res, direction, image, image_halo, sol, scal = rhs, None, None, None, None, None
    for turn in range(1, ITERS):
        first, last = turn == 1, turn == ITERS - 1
        args = (rows, odd, even) + (() if first else (odd_c, even_c)) + (centre, rim, res, halo)
        args += () if first else (direction, image, image_halo, sol, scal)
        state = [line, tile, tile, tile, tile, ((8, LANES), F32)]
        state += [tile] * 2 if last else [((width, 3 * LANES), F32)] + [tile] * 4
        row, res, direction, image, sol, scal, message, centre, *rest = call(
            functools.partial(step_kernel, count, first, last),
            args + (inv, blk) + shared,
            state,
            "apply%d" % turn,
            scratch=[picked, faces, sums],
        )
        if not last:
            rim, halo, image_halo = rest
        odd, even = exchange(message)
        rows = gather_rows(row)
    sol, res = call(
        last_kernel,
        (rows, odd, even, centre, res, direction, image, sol, scal, inv, blk, weight_v, coil_v),
        [tile, tile],
        "finish",
    )
    return sol, res


def solution(mesh):
    return jax.shard_map(
        functools.partial(body, mesh.shape["dom"]),
        mesh=mesh,
        in_specs=(
            P(None, "dom"),
            P(None, "dom"),
            P(None, "dom"),
            P(None, None, None, "dom"),
            P(None, "dom"),
            P(None, "dom"),
            P("dom"),
            P("dom", None),
            P(),
            P(),
            P(),
        ),
        out_specs=(P(None, "dom"), P(None, "dom")),
        check_vma=False,
    )
```
